32 devices in a mesh: grid: 8 (over z, y), probe: 4 (over x, core).
Axes of the slice: x: 2, y: 2, z: 4, core: 2. Of those that a mesh axis runs over, the one named last changes fastest.
Arguments:
- probes: float32 [2048, 8, 2048], P('grid', 'probe'), may hold values from -6 to 6
- corr_lengths: float32 [2], replicated, may hold values from 32 to 256
- footprints: bfloat16 [2048, 16, 128], P('grid'), may hold values from 4.863739e-05 to 0.001953125
- reading_slab: int32 [2048, 1], P('grid'), may hold values from 0 to 7; in each aligned block of 256 rows (0 to 255, 256 to 511, ...) at most 64 rows name the same one
- reading_band: int32 [2048], P('grid'), may hold values from 0 to 15
- reading_tile: int32 [2048], P('grid'), may hold values from 0 to 15
Outputs:
- smoothed: float32 [2048, 8, 2048], P('grid', 'probe')
- sketch: float32 [2048, 8], P('grid', 'probe')
- factor: float32 [8, 8], replicated
- basis: float32 [2048, 8], P('grid', 'probe')
The draws below stay inside these ranges and needn't reach their ends.
Inputs may be any that keep to these rules, and one draw needn't show every extreme that they name: `reading_slab`: among the 256 readings of one owner (aligned blocks of rows), no slab index is named by more than 64 readings, and in every draw some slab index of some owner is named by exactly 64.
All inputs are finite; a program needn't handle non-finite values.
Results may differ from the reference program's by a relative error of at most 0.00065.
Values may be sent and summed in bfloat16 or wider, within the bound.
No kernel may reach another device: no remote copies, remote signals or barrier semaphores. Data moves between devices by JAX's collectives and lax.ppermute only.
A program may use at most 128 MiB of HBM per device.

```python
import math
import jax
import jax.numpy as jnp
import numpy as np
from jax import lax

NY = 2048
NX = 2048
READ_DEV = 256
FR = 16
FC = 128
PROBES = 8
READINGS = 2048
SLABS = 8
SLAB_ROWS = 256
BANDS = 16
TILES = 16
CAP = 64


def touch_ends(values, own_key, least, top_value):
    spot = [jax.random.randint(jax.random.fold_in(own_key, axis), (), 0, length) for axis, length in enumerate(values.shape)]
    longest = values.shape.index(max(values.shape))
    beside = spot[:longest] + [(spot[longest] + 1) % values.shape[longest]] + spot[longest + 1:]
    return values.at[tuple(spot)].set(least).at[tuple(beside)].set(top_value)


def level_of(key, dims, cuts, smallest, largest):
    def one(axis_at, blocks):
        heights = jax.random.uniform(jax.random.fold_in(jax.random.fold_in(key, 6), axis_at), (blocks,), jnp.float32, smallest / len(cuts), largest / len(cuts))
        return jnp.repeat(jnp.exp(heights), dims[axis_at] // blocks).reshape((-1,) + (1,) * (len(dims) - axis_at - 1))

    gain = one(*cuts[0])
    for cut in cuts[1:]:
        gain = gain * one(*cut)
    return gain


def assign_block(key, own, number, rows, number_of, top, limit, slope):
    order = jax.random.permutation(key, number_of)
    crowded, usual = load_shares(number_of, rows * top, limit, slope, True), load_shares(number_of, rows * top, limit, slope, False)
    places = jnp.arange(number_of)

    def named(tallies, offset_by):
        used = int((tallies > 0).sum())
        fixed = max(1, used // 4)
        moved = fixed + (places - fixed + offset_by * (used - fixed)) % max(1, number_of - fixed)
        return jnp.zeros((number_of,), jnp.int32).at[order[jnp.where(places < fixed, places, moved)]].set(jnp.asarray(tallies, jnp.int32))

    tallies = jnp.where(number % 4 == 0, named(crowded, number // 4), named(usual, number - number // 4 - 1))
    mixed = jax.random.permutation(jax.random.fold_in(own, 3), number_of)
    donor, receiver = mixed[0:number_of // 2 * 2:2], mixed[1:number_of // 2 * 2:2]
    room = jnp.minimum(tallies[donor] - 1, limit - tallies[receiver]) // 2
    room = jnp.where((donor == order[0]) | (receiver == order[0]) | (tallies[receiver] == 0), 0, jnp.maximum(room, 0))
    moved = jax.random.randint(jax.random.fold_in(own, 4), (number_of // 2,), 0, 1 << 20) % (room + 1)
    tallies = tallies.at[donor].add(-moved).at[receiver].add(moved)
    members = jnp.searchsorted(jnp.cumsum(tallies), jnp.arange(rows * top), side="right").astype(jnp.int32)
    listing = members.reshape(top, rows).T
    listing = listing[jax.random.permutation(jax.random.fold_in(own, 1), rows)]
    offset_by = jax.random.randint(jax.random.fold_in(own, 2), (rows, 1), 0, top)
    return jnp.take_along_axis(listing, (jnp.arange(top)[None, :] + offset_by) % top, axis=1)


def load_shares(number_of, total, limit, lean, full):
    loads = [(1 << 20) // math.isqrt(grade ** lean) + 1 for grade in range(1, number_of + 1)]
    largest = limit if full else min(limit, max(-(-total // number_of), total * loads[0] // sum(loads)))
    least = 1 if total - largest >= number_of - 1 else 0
    given, rest = [largest] + [least] * (number_of - 1), total - largest - least * (number_of - 1)
    while rest > 0:
        candidates = [i for i in range(1, number_of) if given[i] < largest] or [i for i in range(1, number_of) if given[i] < limit]
        whole, remaining = sum([loads[i] for i in candidates]), rest
        for i in candidates:
            more = min(limit - given[i], max(1, remaining * loads[i] // whole), rest)
            given[i] = given[i] + more
            rest = rest - more
    return np.array(given)


def normal_values(stream_key, shape, deviation, reach, cuts=(), held_as=jnp.bfloat16):
    gain = level_of(stream_key, shape, cuts, -0.22, 0.18) if cuts else 1.0
    entries = jax.random.normal(stream_key, shape, jnp.float32) * deviation * gain
    return jnp.minimum(jnp.maximum(entries, -reach), reach).astype(held_as)


def setup_inputs(seed: int = 0) -> dict:
    seeds = jax.random.split(jax.random.key(seed), 7)
    probes = normal_values(seeds[0], (NY, PROBES, NX), 1.0, 6.0, ((0, 8), (1, 4)), jnp.float32)
    corr_lengths = jnp.clip(jnp.exp(jax.random.uniform(seeds[1], (2,), jnp.float32, math.log(32.0), math.log(256.0))), 32.0, 256.0)
    footprints = jnp.clip(jnp.exp(math.log(0.001953125) - 3.6927934 * jax.random.uniform(seeds[2], (READINGS, FR, FC), jnp.float32) ** level_of(seeds[2], (READINGS, FR, FC), ((0, 8),), -0.2, 0.2)), 4.863739013671875e-05, 0.001953125).astype(jnp.bfloat16)
    reading_slab_keys = jax.random.split(jax.random.fold_in(seeds[3], 1), READINGS // READ_DEV)
    reading_slab_turns = jax.random.permutation(jax.random.fold_in(seeds[3], 3), READINGS // READ_DEV)
    reading_slab = jax.vmap(lambda own, number: assign_block(jax.random.fold_in(seeds[3], 2), own, number, READ_DEV, SLABS, 1, CAP, 2))(reading_slab_keys, reading_slab_turns).reshape((READINGS, 1))
    reading_band = touch_ends(jax.random.randint(seeds[4], (READINGS,), 0, BANDS), jax.random.fold_in(seeds[4], 1), 0, BANDS - 1).astype(jnp.int32)
    reading_tile = touch_ends(jax.random.randint(seeds[5], (READINGS,), 0, TILES), jax.random.fold_in(seeds[5], 1), 0, TILES - 1).astype(jnp.int32)
    return {"probes": probes, "corr_lengths": corr_lengths, "footprints": footprints, "reading_slab": reading_slab, "reading_band": reading_band, "reading_tile": reading_tile}


def wavenumbers(length):
    index_vals = jnp.arange(length, dtype=jnp.int32)
    signed_vals = jnp.where(index_vals < length // 2, index_vals, index_vals - length)
    return signed_vals.astype(jnp.float32) * (2.0 * math.pi / length)

def reference(probes, corr_lengths, footprints, reading_slab, reading_band, reading_tile):
    wave_y = wavenumbers(NY)
    wave_x = wavenumbers(NX)
    spectrum_shape = (1.0 + (corr_lengths[0] * wave_y)[:, None] ** 2 + (corr_lengths[1] * wave_x)[None, :] ** 2) ** (-0.75)
    spectral_filter = spectrum_shape * lax.rsqrt(jnp.mean(spectrum_shape * spectrum_shape))

    def smooth_probe(probe_field):
        spectrum = jnp.fft.fft2(probe_field)
        return jnp.real(jnp.fft.ifft2(spectrum * spectral_filter)).astype(jnp.float32)
    smoothed = jnp.moveaxis(lax.map(smooth_probe, jnp.moveaxis(probes, 1, 0)), 0, 1)
    field_b = smoothed.astype(jnp.bfloat16)
    row_start = (reading_slab[:, 0] * SLAB_ROWS + reading_band * FR).astype(jnp.int32)
    col_start = (reading_tile * FC).astype(jnp.int32)

    def block_reading(footprint, row_at, col_at):
        field_block = lax.dynamic_slice(field_b, (row_at, jnp.int32(0), col_at), (FR, PROBES, FC))
        return jnp.einsum('ab,apb->p', footprint.astype(jnp.float32), field_block.astype(jnp.float32))

    def batch_readings(operands):
        return jax.vmap(block_reading)(operands[0], operands[1], operands[2])
    groups = READINGS // READ_DEV
    sketch = lax.map(batch_readings, (footprints.reshape(groups, READ_DEV, FR, FC), row_start.reshape(groups, READ_DEV), col_start.reshape(groups, READ_DEV))).reshape(READINGS, PROBES)
    gram = jnp.dot(sketch.T, sketch, precision=lax.Precision.HIGHEST) / READINGS
    lower_factor = jnp.linalg.cholesky(gram)
    factor = lower_factor.T
    basis = jax.scipy.linalg.solve_triangular(lower_factor, sketch.T, lower=True).T
    return (smoothed, sketch, factor, basis)
```

```python
import math

import jax
import jax.numpy as jnp
import ml_dtypes
import numpy as np
from jax import lax
from jax.experimental import pallas as pl
from jax.experimental.pallas import tpu as pltpu
from jax.sharding import PartitionSpec as P

RADIX = 8
STEPS = 64.0
TOP = 32700.0
TILE = 64
SUB = 16
LANES = 128
F32 = jnp.float32
BF16 = jnp.bfloat16
I16 = jnp.int16


def dft_blocks(length):
    grid = np.outer(np.arange(length), np.arange(length)) % length
    cosine, sine = np.cos(2 * np.pi * grid / length), np.sin(2 * np.pi * grid / length)
    forward = np.block([[cosine, -sine], [sine, cosine]]).astype(np.float32)
    lead = forward.astype(ml_dtypes.bfloat16)
    trail = (forward - lead.astype(np.float32)).astype(ml_dtypes.bfloat16)
    return lead, trail, lead.T.copy(), trail.T.copy()


def twiddles(length):
    short = length // RADIX
    angle = 2 * np.pi * np.outer(np.arange(RADIX), np.arange(short)) / length
    return np.concatenate([np.cos(angle), -np.sin(angle)]).astype(np.float32)


def turn(pair, sign):
    return (pair[1], -pair[0]) if sign < 0 else (-pair[1], pair[0])


def add(one, two):
    return (one[0] + two[0], one[1] + two[1])


def sub(one, two):
    return (one[0] - two[0], one[1] - two[1])


def dft8(x, sign):
    half = math.sqrt(0.5)
    a0, a1 = add(x[0], x[4]), sub(x[0], x[4])
    a2, a3 = add(x[2], x[6]), turn(sub(x[2], x[6]), sign)
    b0, b1 = add(x[1], x[5]), sub(x[1], x[5])
    b2, b3 = add(x[3], x[7]), turn(sub(x[3], x[7]), sign)
    even, odd = add(a0, a2), add(b0, b2)
    side, cross = sub(a0, a2), turn(sub(b0, b2), sign)
    c1, d1 = add(a1, a3), add(b1, b3)
    c3, d3 = sub(a1, a3), sub(b1, b3)
    t1, t3 = turn(d1, sign), turn(d3, sign)
    w1 = (half * (d1[0] + t1[0]), half * (d1[1] + t1[1]))
    w3 = (half * (t3[0] - d3[0]), half * (t3[1] - d3[1]))
    return [
        add(even, odd), add(c1, w1), add(side, cross), add(c3, w3),
        sub(even, odd), sub(c1, w1), sub(side, cross), sub(c3, w3),
    ]


def spin(pair, cosine, sine):
    return (pair[0] * cosine - pair[1] * sine, pair[0] * sine + pair[1] * cosine)


def split(value):
    lead = value.astype(BF16)
    return lead, (value - lead.astype(F32)).astype(BF16)


def dot(one, two):
    return jnp.dot(one, two, preferred_element_type=F32)


def encode(value):
    top = jnp.maximum(jnp.max(jnp.abs(value), axis=0, keepdims=True), 1e-30)
    exponent = jnp.ceil(jnp.log2(top) * STEPS)
    code = jnp.round(value * (jnp.exp2(exponent * (-1.0 / STEPS)) * TOP))
    return code.astype(jnp.int32).astype(I16), exponent


def scales(exponent):
    return jnp.exp2(exponent.astype(jnp.int32).astype(F32) * (1.0 / STEPS)) * (1.0 / TOP)


def rows_kernel(slabs, chunks, me_ref, x_ref, lead_ref, trail_ref, turn_ref, *rest):
    outs, (stack, marks, high, low) = rest[: slabs * chunks], rest[slabs * chunks:]
    step, last = pl.program_id(0), pl.num_programs(0) - 1
    short = turn_ref.shape[1]
    halves, tile = short // LANES, high.shape[0] // RADIX
    rows = (outs[0].shape[0] - RADIX) // 2
    width = outs[0].shape[1]
    stride = 2 * RADIX * halves
    for start in range(0, tile, SUB):
        for half in range(halves):
            values = []
            for n1 in range(RADIX):
                at = start * stride + (n1 * halves + half) * 2
                values.append(
                    tuple(x_ref[pl.ds(at + part, SUB, stride=stride), :] for part in range(2))
                )
            mixed = dft8(values, -1)
            for k1 in range(RADIX):
                lanes = slice(half * LANES, (half + 1) * LANES)
                pair = mixed[k1]
                if k1:
                    pair = spin(
                        pair, turn_ref[k1:k1 + 1, lanes], turn_ref[RADIX + k1:RADIX + k1 + 1, lanes]
                    )
                for part in range(2):
                    at = part * short + half * LANES
                    lead, trail = split(pair[part])
                    high[k1 * tile + start:k1 * tile + start + SUB, at:at + LANES] = lead
                    low[k1 * tile + start:k1 * tile + start + SUB, at:at + LANES] = trail
    spectrum = (
        dot(high[...], lead_ref[...]) + dot(low[...], lead_ref[...]) + dot(high[...], trail_ref[...])
    )
    own = short * RADIX // slabs
    for slab in range(slabs):
        k1, base = slab * own // short, slab * own % short
        for chunk in range(chunks):
            for part in range(2):
                at = part * short + base + chunk * width
                code, exponent = encode(
                    spectrum[k1 * tile:(k1 + 1) * tile, at:at + width]
                )
                place = pl.multiple_of(part * rows + step * tile, SUB)
                stack[chunk, slab, pl.ds(place, tile), :] = code
                marks[chunk, slab, pl.ds(2 * step + part, 1), :] = exponent

    @pl.when(step == last)
    def _():
        for chunk in range(chunks):
            for hop in range(slabs):
                slab = me_ref[0] ^ hop
                out = outs[chunk * slabs + hop]
                out[:2 * rows, :] = stack[chunk, slab]
                out[2 * rows:, :] = marks[chunk, slab].astype(jnp.int32).astype(I16)


def columns_kernel(slabs, chunk, length, me_ref, corr_ref, *rest):
    ins, rest = rest[:slabs], rest[slabs:]
    back_lead, back_trail, lead, trail, turn_ref = rest[:5]
    outs, (stack, scale, field, high, low) = rest[5:5 + slabs], rest[5 + slabs:]
    me = me_ref[0]
    short = length // RADIX
    rows = stack.shape[1] // 2
    width = stack.shape[2]
    tile = min(TILE, rows)
    group = high.shape[2] // width
    for hop in range(slabs):
        stack[me ^ hop] = ins[hop][:2 * rows, :]
        scale[me ^ hop] = scales(ins[hop][2 * rows:, :])
    for start in range(0, short, SUB):
        values = []
        for n1 in range(RADIX):
            slab, row = divmod(n1 * short + start, rows)
            mark = 2 * (row // tile)
            values.append(
                tuple(
                    stack[slab, part * rows + row:part * rows + row + SUB, :].astype(jnp.int32).astype(F32)
                    * scale[slab, mark + part:mark + part + 1, :]
                    for part in range(2)
                )
            )
        mixed = dft8(values, -1)
        for k1 in range(RADIX):
            pair = mixed[k1]
            if k1:
                pair = spin(
                    pair,
                    turn_ref[start:start + SUB, k1:k1 + 1],
                    turn_ref[start:start + SUB, RADIX + k1:RADIX + k1 + 1],
                )
            at = (k1 % group) * width
            for part in range(2):
                one, two = split(pair[part])
                place = slice(part * short + start, part * short + start + SUB)
                high[k1 // group, place, at:at + width] = one
                low[k1 // group, place, at:at + width] = two
    place = me * (length // slabs) + chunk * width
    lane = place + lax.broadcasted_iota(jnp.int32, (1, width), 1)
    wave_x = (lane // short) + RADIX * (lane % short)
    wave_x = jnp.where(wave_x < length // 2, wave_x, wave_x - length).astype(F32)
    unit = 2.0 * math.pi / length
    across = (corr_ref[1] * (wave_x * unit)) ** 2 + 1.0
    count = lax.broadcasted_iota(jnp.int32, (short, 1), 0)
    for pair_at in range(RADIX // group):
        one, two = high[pair_at], low[pair_at]
        spectrum = dot(lead[...], one) + dot(lead[...], two) + dot(trail[...], one)
        for slot in range(group):
            k1 = pair_at * group + slot
            wave_y = k1 + RADIX * count
            wave_y = jnp.where(wave_y < length // 2, wave_y, wave_y - length).astype(F32)
            down = (corr_ref[0] * (wave_y * unit)) ** 2
            root = lax.rsqrt(down + across)
            shape = root * root * lax.rsqrt(root)
            lanes = slice(slot * width, (slot + 1) * width)
            for part in range(2):
                place = slice(part * short, (part + 1) * short)
                one, two = split(spectrum[place, lanes] * shape)
                high[pair_at, place, lanes] = one
                low[pair_at, place, lanes] = two
        one, two = high[pair_at], low[pair_at]
        spectrum = (
            dot(back_lead[...], one) + dot(back_lead[...], two) + dot(back_trail[...], one)
        )
        for slot in range(group):
            k1 = pair_at * group + slot
            lanes = slice(slot * width, (slot + 1) * width)
            pair = (spectrum[:short, lanes], spectrum[short:, lanes])
            if k1:
                pair = spin(
                    pair, turn_ref[:, k1:k1 + 1], -turn_ref[:, RADIX + k1:RADIX + k1 + 1]
                )
            for part in range(2):
                field[part, k1 * short:(k1 + 1) * short, :] = pair[part]
    for start in range(0, short, SUB):
        values = [
            tuple(
                field[part, k1 * short + start:k1 * short + start + SUB, :] for part in range(2)
            )
            for k1 in range(RADIX)
        ]
        mixed = dft8(values, 1)
        for n1 in range(RADIX):
            for part in range(2):
                field[part, n1 * short + start:n1 * short + start + SUB, :] = mixed[n1][part]
    for slab in range(slabs):
        for at in range(rows // tile):
            for part in range(2):
                begin = slab * rows + at * tile
                code, exponent = encode(field[part, begin:begin + tile, :])
                stack[slab, part * rows + at * tile:part * rows + (at + 1) * tile, :] = code
                scale[slab, 2 * at + part:2 * at + part + 1, :] = exponent
    for hop in range(slabs):
        outs[hop][:2 * rows, :] = stack[me ^ hop]
        outs[hop][2 * rows:, :] = scale[me ^ hop].astype(jnp.int32).astype(I16)


def finish_kernel(slabs, chunks, me_ref, gain_ref, *rest):
    ins, rest = rest[:slabs * chunks], rest[slabs * chunks:]
    lead_ref, trail_ref, turn_ref, prints_ref, index_ref, out_ref, value_ref = rest[:7]
    stack, scale, high, low, field, blocks = rest[7:]
    step, last = pl.program_id(0), pl.num_programs(0) - 1
    short = turn_ref.shape[1]
    halves, tile = short // LANES, high.shape[0] // RADIX
    rows = stack.shape[2] // 2
    width = stack.shape[3]
    stride = 2 * RADIX * halves

    @pl.when(step == 0)
    def _():
        for chunk in range(chunks):
            for hop in range(slabs):
                slab = me_ref[0] ^ hop
                stack[chunk, slab] = ins[chunk * slabs + hop][:2 * rows, :]
                scale[chunk, slab] = scales(ins[chunk * slabs + hop][2 * rows:, :])

    own = short * RADIX // slabs
    for slab in range(slabs):
        k1, base = slab * own // short, slab * own % short
        for chunk in range(chunks):
            for part in range(2):
                place = pl.multiple_of(part * rows + step * tile, SUB)
                value = (
                    stack[chunk, slab, pl.ds(place, tile), :].astype(jnp.int32).astype(F32)
                    * scale[chunk, slab, pl.ds(2 * step + part, 1), :]
                )
                at = part * short + base + chunk * width
                one, two = split(value)
                high[k1 * tile:(k1 + 1) * tile, at:at + width] = one
                low[k1 * tile:(k1 + 1) * tile, at:at + width] = two
    mixed = (
        dot(high[...], lead_ref[...]) + dot(low[...], lead_ref[...]) + dot(high[...], trail_ref[...])
    )
    gain = gain_ref[0]
    for start in range(0, tile, SUB):
        for half in range(halves):
            lanes = slice(half * LANES, (half + 1) * LANES)
            values = []
            for k1 in range(RADIX):
                place = slice(k1 * tile + start, k1 * tile + start + SUB)
                at = half * LANES
                pair = (mixed[place, at:at + LANES], mixed[place, short + at:short + at + LANES])
                if k1:
                    pair = spin(
                        pair, turn_ref[k1:k1 + 1, lanes], -turn_ref[RADIX + k1:RADIX + k1 + 1, lanes]
                    )
                values.append(pair)
            done = dft8(values, 1)
            for n1 in range(RADIX):
                column = n1 * halves + half
                for part in range(2):
                    value = done[n1][part] * gain
                    out_ref[pl.ds(start * stride + column * 2 + part, SUB, stride=stride), :] = value
                    place = pl.multiple_of(step * tile + start, SUB)
                    field[part * RADIX * halves + column, pl.ds(place, SUB), :] = value

    @pl.when(step == last)
    def _():
        band_rows = prints_ref.shape[0] // LANES
        bands = field.shape[1] // band_rows
        count = field.shape[0]
        for column in range(count):
            for row in range(band_rows):
                piece = field[column, pl.ds(row, bands, stride=band_rows), :]
                blocks[column * bands:(column + 1) * bands, row * LANES:(row + 1) * LANES] = (
                    piece.astype(BF16)
                )
        values = dot(blocks[...], prints_ref[...])
        each = count // 2 * bands
        chosen = lax.broadcasted_iota(jnp.int32, (each, 1), 0) == index_ref[...]
        for part in range(2):
            value_ref[part:part + 1, :] = jnp.sum(
                jnp.where(chosen, values[part * each:(part + 1) * each, :], 0.0), axis=0, keepdims=True
            )


def pack_kernel(source_ref, prints_ref, out_ref, semaphore):
    out_ref[...] = jnp.zeros_like(out_ref)
    count = out_ref.shape[0]

    def begin(at, carry):
        @pl.when(source_ref[at] >= 0)
        def _():
            pltpu.make_async_copy(
                prints_ref.at[source_ref[at]], out_ref.at[at], semaphore
            ).start()
        return carry

    def end(at, carry):
        @pl.when(source_ref[at] >= 0)
        def _():
            pltpu.make_async_copy(
                prints_ref.at[source_ref[at]], out_ref.at[at], semaphore
            ).wait()
        return carry

    lax.fori_loop(0, count, begin, 0)
    lax.fori_loop(0, count, end, 0)


def small_kernel(slabs, lanes_q, each, total, row_ref, all_ref, pick_ref, sketch_ref, factor_ref, basis_ref, own):
    probes = lanes_q * each
    tiles = all_ref.shape[1] // each
    gram = {}
    for one in range(probes):
        for two in range(one + 1):
            sum_here = None
            for slab in range(slabs):
                left = all_ref[slab * lanes_q + one // each, (one % each) * tiles:(one % each + 1) * tiles, :]
                right = all_ref[slab * lanes_q + two // each, (two % each) * tiles:(two % each + 1) * tiles, :]
                term = left * right
                sum_here = term if sum_here is None else sum_here + term
            sum_here = jnp.sum(jnp.sum(sum_here, axis=0, keepdims=True), axis=1, keepdims=True)
            gram[one, two] = sum_here * (1.0 / total)
    lower, inverse = {}, {}
    for at in range(probes):
        left = gram[at, at]
        for back in range(at):
            left = left - lower[at, back] * lower[at, back]
        root = jnp.sqrt(left)
        lower[at, at] = root
        inverse[at] = 1.0 / root
        for down in range(at + 1, probes):
            value = gram[down, at]
            for back in range(at):
                value = value - lower[down, back] * lower[at, back]
            lower[down, at] = value * inverse[at]
    row = lax.broadcasted_iota(jnp.int32, (probes, probes), 0)
    column = lax.broadcasted_iota(jnp.int32, (probes, probes), 1)
    factor = jnp.zeros((probes, probes), F32)
    for one in range(probes):
        for two in range(one + 1):
            factor = jnp.where((row == two) & (column == one), lower[one, two], factor)
    factor_ref[...] = factor
    for slab in range(slabs):
        for one in range(probes):
            own[one:one + 1, slab * LANES:(slab + 1) * LANES] = all_ref[
                slab * lanes_q + one // each, pl.ds((one % each) * tiles + row_ref[0], 1), :
            ]
    value = own[...]
    first = value.astype(BF16)
    rest = value - first.astype(F32)
    second = rest.astype(BF16)
    third = (rest - second.astype(F32)).astype(BF16)
    sketch = dot(first, pick_ref[...]) + dot(second, pick_ref[...]) + dot(third, pick_ref[...])
    sketch_ref[...] = sketch
    solved = []
    for at in range(probes):
        value = sketch[at:at + 1, :]
        for back in range(at):
            value = value - lower[at, back] * solved[back]
        solved.append(value * inverse[at])
        basis_ref[at:at + 1, :] = solved[at]


def vmem():
    return pl.BlockSpec(memory_space=pltpu.VMEM)


def smem():
    return pl.BlockSpec(memory_space=pltpu.SMEM)


def params():
    return pltpu.CompilerParams(vmem_limit_bytes=56 << 20)


def filter_power(corr_lengths, height, width):
    wave_y = jnp.arange(height // 2 + 1, dtype=jnp.int32)
    wave_x = jnp.arange(width // 2 + 1, dtype=jnp.int32)
    weight_y = jnp.where((wave_y == 0) | (wave_y == height // 2), 1.0, 2.0)
    weight_x = jnp.where((wave_x == 0) | (wave_x == width // 2), 1.0, 2.0)
    down = (corr_lengths[0] * (wave_y.astype(F32) * (2.0 * math.pi / height))) ** 2
    across = (corr_lengths[1] * (wave_x.astype(F32) * (2.0 * math.pi / width))) ** 2
    root = lax.rsqrt(1.0 + down[:, None] + across[None, :])
    return jnp.sum(root * root * root * (weight_y[:, None] * weight_x[None, :]))


def exchange(blocks):
    slabs = len(blocks)
    order = sorted(range(1, slabs), key=lambda hop: (-(hop * 2 // slabs), -(hop * 4 // slabs % 2)))
    arrived = [blocks[0]] + [None] * (slabs - 1)
    for hop in order:
        pairs = [(source, source ^ hop) for source in range(slabs)]
        arrived[hop] = lax.ppermute(blocks[hop], "grid", pairs)
    return arrived


def local(probes, corr_lengths, footprints, reading_slab, reading_band, reading_tile):
    rows, each, width = probes.shape
    slabs, lanes_q = lax.axis_size("grid"), lax.axis_size("probe")
    me, lane_at = lax.axis_index("grid"), lax.axis_index("probe")
    height = rows * slabs
    short = width // RADIX
    own = width // slabs
    cut = min(LANES, own)
    chunks = own // cut
    tile = min(TILE, rows)
    halves = short // LANES
    lead, trail, back_lead, back_trail = (jnp.asarray(part) for part in dft_blocks(short))
    turn_x = jnp.asarray(twiddles(width))
    turn_y = jnp.asarray(twiddles(height).T.copy())
    me_list = me.reshape(1).astype(jnp.int32)
    column_tiles = width // LANES
    flat = (
        probes.reshape(rows, each, column_tiles, LANES)
        .transpose(0, 2, 1, 3)
        .reshape(rows * each * column_tiles, LANES)
    )
    payload = jax.ShapeDtypeStruct((2 * rows + RADIX, cut), I16)

    def whole(shape):
        return pl.BlockSpec(shape, lambda step: (0,) * len(shape))

    sent = pl.pallas_call(
        lambda *refs: rows_kernel(slabs, chunks, *refs),
        grid=(rows // tile,),
        in_specs=[
            smem(),
            pl.BlockSpec((tile * each * column_tiles, LANES), lambda step: (step, 0)),
            whole(lead.shape),
            whole(trail.shape),
            whole(turn_x.shape),
        ],
        out_specs=[whole(payload.shape)] * (chunks * slabs),
        out_shape=[payload] * (chunks * slabs),
        scratch_shapes=[
            pltpu.VMEM((chunks, slabs, 2 * rows, cut), I16),
            pltpu.VMEM((chunks, slabs, RADIX, cut), F32),
            pltpu.VMEM((RADIX * tile, 2 * short), BF16),
            pltpu.VMEM((RADIX * tile, 2 * short), BF16),
        ],
        compiler_params=params(),
        name="rows_forward",
    )(me_list, flat, lead, trail, turn_x)

    arrived = []
    for chunk in range(chunks):
        arrived.append(exchange(sent[chunk * slabs:(chunk + 1) * slabs]))

    read_count, band_rows, tile_cols = footprints.shape
    band_count = rows // band_rows
    tile_count = width // tile_cols
    capacity = 2 * read_count // slabs
    share = capacity // lanes_q
    target = reading_slab[:, 0]
    reading = jnp.arange(read_count, dtype=jnp.int32)
    onehot = (target[:, None] == jnp.arange(slabs, dtype=jnp.int32)[None, :]).astype(F32)
    before = (reading[:, None] > reading[None, :]).astype(F32)
    slot = jnp.sum(jnp.dot(before, onehot) * onehot, axis=1).astype(jnp.int32)
    place = target * capacity + slot
    code = reading_tile * band_count + reading_band
    wanted = (
        jnp.arange(slabs, dtype=jnp.int32)[:, None] * capacity
        + lane_at * share
        + jnp.arange(share, dtype=jnp.int32)[None, :]
    ).reshape(-1)
    source = jnp.max(
        jnp.where(wanted[:, None] == place[None, :], reading[None, :], -1), axis=1
    )
    packed = pl.pallas_call(
        pack_kernel,
        in_specs=[smem(), pl.BlockSpec(memory_space=pl.ANY)],
        out_specs=vmem(),
        out_shape=jax.ShapeDtypeStruct((slabs * share, band_rows, tile_cols), BF16),
        scratch_shapes=[pltpu.SemaphoreType.DMA],
        compiler_params=params(),
        name="pack_prints",
    )(source, footprints)
    shared = lax.all_to_all(
        packed.reshape(slabs, share, band_rows, tile_cols), "grid", split_axis=0, concat_axis=0, tiled=True
    )
    prints = lax.all_gather(shared, "probe", axis=0, tiled=False)
    slots = slabs * capacity
    prints = prints.transpose(3, 4, 1, 0, 2).reshape(band_rows * tile_cols, slots)
    listed = lax.all_gather(jnp.stack([place, code]), "grid", axis=0, tiled=False)
    here = me * capacity + jnp.arange(capacity, dtype=jnp.int32)
    index = jnp.max(
        jnp.where(here[None, :, None] == listed[:, 0, None, :], listed[:, 1, None, :], 0), axis=2
    ).reshape(1, slots)

    gain = lax.rsqrt(filter_power(corr_lengths, height, width) / (height * width)) / (height * width)

    returned = []
    group = 256 // cut if cut % LANES == 0 else 1
    for chunk in range(chunks):
        results = pl.pallas_call(
            lambda *refs, chunk=chunk: columns_kernel(slabs, chunk, height, *refs),
            in_specs=[smem(), smem()] + [vmem()] * (slabs + 5),
            out_specs=[vmem()] * slabs,
            out_shape=[payload] * slabs,
            scratch_shapes=[
                pltpu.VMEM((slabs, 2 * rows, cut), I16),
                pltpu.VMEM((slabs, RADIX, cut), F32),
                pltpu.VMEM((2, height, cut), F32),
                pltpu.VMEM((RADIX // group, 2 * short, group * cut), BF16),
                pltpu.VMEM((RADIX // group, 2 * short, group * cut), BF16),
            ],
            compiler_params=params(),
            name="columns",
        )(me_list, corr_lengths, *arrived[chunk], lead, trail, back_lead, back_trail, turn_y)
        returned += exchange(results)

    smoothed, values = pl.pallas_call(
        lambda *refs: finish_kernel(slabs, chunks, *refs),
        grid=(rows // tile,),
        in_specs=[smem(), smem()]
        + [whole(payload.shape)] * (chunks * slabs)
        + [
            whole(lead.shape),
            whole(trail.shape),
            whole(turn_x.shape),
            whole(prints.shape),
            whole(index.shape),
        ],
        out_specs=[
            pl.BlockSpec((tile * each * column_tiles, LANES), lambda step: (step, 0)),
            whole((each, slots)),
        ],
        out_shape=[
            jax.ShapeDtypeStruct(flat.shape, F32),
            jax.ShapeDtypeStruct((each, slots), F32),
        ],
        scratch_shapes=[
            pltpu.VMEM((chunks, slabs, 2 * rows, cut), I16),
            pltpu.VMEM((chunks, slabs, RADIX, cut), F32),
            pltpu.VMEM((RADIX * tile, 2 * short), BF16),
            pltpu.VMEM((RADIX * tile, 2 * short), BF16),
            pltpu.VMEM((each * column_tiles, rows, LANES), F32),
            pltpu.VMEM((each * column_tiles * band_count, band_rows * tile_cols), BF16),
        ],
        compiler_params=params(),
        name="rows_back",
    )(me_list, gain.reshape(1), *returned, back_lead, back_trail, turn_x, prints, index)
    smoothed = (
        smoothed.reshape(rows, column_tiles, each, LANES).transpose(0, 2, 1, 3).reshape(rows, each, width)
    )

    group_count = slabs * lanes_q
    spread = jnp.broadcast_to(
        values.reshape(1, each * slots // LANES, LANES), (group_count, each * slots // LANES, LANES)
    )
    everyone = lax.all_to_all(spread, ("grid", "probe"), split_axis=0, concat_axis=0, tiled=True)
    offset = me * capacity
    lane_of = target * LANES + offset % LANES + slot
    pick = (jnp.arange(slabs * LANES, dtype=jnp.int32)[:, None] == lane_of[None, :]).astype(BF16)
    probe_count = each * lanes_q
    full, factor, basis = pl.pallas_call(
        lambda *refs: small_kernel(slabs, lanes_q, each, read_count * slabs, *refs),
        in_specs=[smem(), vmem(), vmem()],
        out_specs=[vmem()] * 3,
        out_shape=[
            jax.ShapeDtypeStruct((probe_count, read_count), F32),
            jax.ShapeDtypeStruct((probe_count, probe_count), F32),
            jax.ShapeDtypeStruct((probe_count, read_count), F32),
        ],
        scratch_shapes=[pltpu.VMEM((probe_count, slabs * LANES), F32)],
        compiler_params=params(),
        name="factor_basis",
    )((offset // LANES).reshape(1), everyone, pick)
    sketch = lax.dynamic_slice_in_dim(full, lane_at * each, each, 0).T
    basis = lax.dynamic_slice_in_dim(basis, lane_at * each, each, 0).T
    return (smoothed, sketch, factor, basis)


def solution(mesh):
    in_specs = (
        P("grid", "probe", None),
        P(),
        P("grid", None, None),
        P("grid", None),
        P("grid"),
        P("grid"),
    )
    out_specs = (P("grid", "probe", None), P("grid", "probe"), P(), P("grid", "probe"))
    return jax.shard_map(local, mesh=mesh, in_specs=in_specs, out_specs=out_specs, check_vma=False)
```

```python
import math

import jax
import jax.numpy as jnp
import ml_dtypes
import numpy as np
from jax import lax
from jax.experimental import pallas as pl
from jax.experimental.pallas import tpu as pltpu
from jax.sharding import PartitionSpec as P

RADIX = 8
STEPS = 64.0
TOP = 32700.0
TILE = 64
SUB = 16
LANES = 128
WINDOW = 5
F32 = jnp.float32
BF16 = jnp.bfloat16
I16 = jnp.int16


def dft_blocks(length):
    grid = np.outer(np.arange(length), np.arange(length)) % length
    cosine, sine = np.cos(2 * np.pi * grid / length), np.sin(2 * np.pi * grid / length)
    forward = np.block([[cosine, -sine], [sine, cosine]]).astype(np.float32)
    lead = forward.astype(ml_dtypes.bfloat16)
    trail = (forward - lead.astype(np.float32)).astype(ml_dtypes.bfloat16)
    return lead, trail, lead.T.copy(), trail.T.copy()


def twiddles(length):
    short = length // RADIX
    angle = 2 * np.pi * np.outer(np.arange(RADIX), np.arange(short)) / length
    return np.concatenate([np.cos(angle), -np.sin(angle)]).astype(np.float32)


def turn(pair, sign):
    return (pair[1], -pair[0]) if sign < 0 else (-pair[1], pair[0])


def add(one, two):
    return (one[0] + two[0], one[1] + two[1])


def sub(one, two):
    return (one[0] - two[0], one[1] - two[1])


def dft8(x, sign):
    half = math.sqrt(0.5)
    a0, a1 = add(x[0], x[4]), sub(x[0], x[4])
    a2, a3 = add(x[2], x[6]), turn(sub(x[2], x[6]), sign)
    b0, b1 = add(x[1], x[5]), sub(x[1], x[5])
    b2, b3 = add(x[3], x[7]), turn(sub(x[3], x[7]), sign)
    even, odd = add(a0, a2), add(b0, b2)
    side, cross = sub(a0, a2), turn(sub(b0, b2), sign)
    c1, d1 = add(a1, a3), add(b1, b3)
    c3, d3 = sub(a1, a3), sub(b1, b3)
    t1, t3 = turn(d1, sign), turn(d3, sign)
    w1 = (half * (d1[0] + t1[0]), half * (d1[1] + t1[1]))
    w3 = (half * (t3[0] - d3[0]), half * (t3[1] - d3[1]))
    return [
        add(even, odd), add(c1, w1), add(side, cross), add(c3, w3),
        sub(even, odd), sub(c1, w1), sub(side, cross), sub(c3, w3),
    ]


def spin(pair, cosine, sine):
    return (pair[0] * cosine - pair[1] * sine, pair[0] * sine + pair[1] * cosine)


def split(value):
    lead = value.astype(BF16)
    return lead, (value - lead.astype(F32)).astype(BF16)


def dot(one, two):
    return jnp.dot(one, two, preferred_element_type=F32)


def encode(value):
    top = jnp.maximum(jnp.max(jnp.abs(value), axis=0, keepdims=True), 1e-30)
    exponent = jnp.ceil(jnp.log2(top) * STEPS)
    code = jnp.round(value * (jnp.exp2(exponent * (-1.0 / STEPS)) * TOP))
    return code.astype(jnp.int32).astype(I16), exponent


def scales(exponent):
    return jnp.exp2(exponent.astype(jnp.int32).astype(F32) * (1.0 / STEPS)) * (1.0 / TOP)


def rows_kernel(slabs, chunks, me_ref, x_ref, lead_ref, trail_ref, turn_ref, *rest):
    outs, (stack, marks, high, low) = rest[: slabs * chunks], rest[slabs * chunks:]
    step, last = pl.program_id(0), pl.num_programs(0) - 1
    short = turn_ref.shape[1]
    halves, tile = short // LANES, high.shape[0] // RADIX
    rows = (outs[0].shape[0] - RADIX) // 2
    width = outs[0].shape[1]
    stride = 2 * RADIX * halves
    for start in range(0, tile, SUB):
        for half in range(halves):
            values = []
            for n1 in range(RADIX):
                at = start * stride + (n1 * halves + half) * 2
                values.append(
                    tuple(x_ref[pl.ds(at + part, SUB, stride=stride), :] for part in range(2))
                )
            mixed = dft8(values, -1)
            for k1 in range(RADIX):
                lanes = slice(half * LANES, (half + 1) * LANES)
                pair = mixed[k1]
                if k1:
                    pair = spin(
                        pair, turn_ref[k1:k1 + 1, lanes], turn_ref[RADIX + k1:RADIX + k1 + 1, lanes]
                    )
                for part in range(2):
                    at = part * short + half * LANES
                    lead, trail = split(pair[part])
                    high[k1 * tile + start:k1 * tile + start + SUB, at:at + LANES] = lead
                    low[k1 * tile + start:k1 * tile + start + SUB, at:at + LANES] = trail
    spectrum = (
        dot(high[...], lead_ref[...]) + dot(low[...], lead_ref[...]) + dot(high[...], trail_ref[...])
    )
    own = short * RADIX // slabs
    for slab in range(slabs):
        k1, base = slab * own // short, slab * own % short
        for chunk in range(chunks):
            for part in range(2):
                at = part * short + base + chunk * width
                code, exponent = encode(
                    spectrum[k1 * tile:(k1 + 1) * tile, at:at + width]
                )
                place = pl.multiple_of(part * rows + step * tile, SUB)
                stack[chunk, slab, pl.ds(place, tile), :] = code
                marks[chunk, slab, pl.ds(2 * step + part, 1), :] = exponent

    @pl.when(step == last)
    def _():
        for chunk in range(chunks):
            for hop in range(slabs):
                slab = me_ref[0] ^ hop
                out = outs[chunk * slabs + hop]
                out[:2 * rows, :] = stack[chunk, slab]
                out[2 * rows:, :] = marks[chunk, slab].astype(jnp.int32).astype(I16)


def pack_copies(slabs, me, source_ref, prints_ref, packed, semaphore, act):
    for hop in range(slabs):
        share = packed[hop].shape[0] - 1

        def one(at, carry, hop=hop, share=share):
            source = source_ref[(me ^ hop) * share + at]

            @pl.when(source >= 0)
            def _():
                act(pltpu.make_async_copy(prints_ref.at[source], packed[hop].at[at], semaphore))

            return carry

        lax.fori_loop(0, share, one, 0)


def columns_kernel(slabs, chunk, length, packs, me_ref, corr_ref, *rest):
    me = me_ref[0]
    if packs:
        (source_ref, prints_ref, code_ref), rest = rest[:3], rest[3:]
        packed, semaphore = rest[-6 - slabs:-6], rest[-6]
        rest = rest[:-6 - slabs] + rest[-5:]
        for hop in range(slabs):
            share = packed[hop].shape[0] - 1
            packed[hop][:share] = jnp.zeros_like(packed[hop][:share])
            packed[hop][share] = code_ref[me ^ hop]
        pack_copies(
            slabs, me, source_ref, prints_ref, packed, semaphore, lambda copy: copy.start()
        )
    ins, rest = rest[:slabs], rest[slabs:]
    back_lead, back_trail, lead, trail, turn_ref = rest[:5]
    outs, (stack, scale, field, high, low) = rest[5:5 + slabs], rest[5 + slabs:]
    short = length // RADIX
    rows = stack.shape[1] // 2
    width = stack.shape[2]
    tile = min(TILE, rows)
    group = high.shape[2] // width
    for hop in range(slabs):
        stack[me ^ hop] = ins[hop][:2 * rows, :]
        scale[me ^ hop] = scales(ins[hop][2 * rows:, :])
    for start in range(0, short, SUB):
        values = []
        for n1 in range(RADIX):
            slab, row = divmod(n1 * short + start, rows)
            mark = 2 * (row // tile)
            values.append(
                tuple(
                    stack[slab, part * rows + row:part * rows + row + SUB, :].astype(jnp.int32).astype(F32)
                    * scale[slab, mark + part:mark + part + 1, :]
                    for part in range(2)
                )
            )
        mixed = dft8(values, -1)
        for k1 in range(RADIX):
            pair = mixed[k1]
            if k1:
                pair = spin(
                    pair,
                    turn_ref[start:start + SUB, k1:k1 + 1],
                    turn_ref[start:start + SUB, RADIX + k1:RADIX + k1 + 1],
                )
            at = (k1 % group) * width
            for part in range(2):
                one, two = split(pair[part])
                place = slice(part * short + start, part * short + start + SUB)
                high[k1 // group, place, at:at + width] = one
                low[k1 // group, place, at:at + width] = two
    place = me * (length // slabs) + chunk * width
    lane = place + lax.broadcasted_iota(jnp.int32, (1, width), 1)
    wave_x = (lane // short) + RADIX * (lane % short)
    wave_x = jnp.where(wave_x < length // 2, wave_x, wave_x - length).astype(F32)
    unit = 2.0 * math.pi / length
    across = (corr_ref[1] * (wave_x * unit)) ** 2 + 1.0
    count = lax.broadcasted_iota(jnp.int32, (short, 1), 0)
    for pair_at in range(RADIX // group):
        one, two = high[pair_at], low[pair_at]
        spectrum = dot(lead[...], one) + dot(lead[...], two) + dot(trail[...], one)
        for slot in range(group):
            k1 = pair_at * group + slot
            wave_y = k1 + RADIX * count
            wave_y = jnp.where(wave_y < length // 2, wave_y, wave_y - length).astype(F32)
            down = (corr_ref[0] * (wave_y * unit)) ** 2
            root = lax.rsqrt(down + across)
            shape = root * root * lax.rsqrt(root)
            lanes = slice(slot * width, (slot + 1) * width)
            for part in range(2):
                place = slice(part * short, (part + 1) * short)
                one, two = split(spectrum[place, lanes] * shape)
                high[pair_at, place, lanes] = one
                low[pair_at, place, lanes] = two
        one, two = high[pair_at], low[pair_at]
        spectrum = (
            dot(back_lead[...], one) + dot(back_lead[...], two) + dot(back_trail[...], one)
        )
        for slot in range(group):
            k1 = pair_at * group + slot
            lanes = slice(slot * width, (slot + 1) * width)
            pair = (spectrum[:short, lanes], spectrum[short:, lanes])
            if k1:
                pair = spin(
                    pair, turn_ref[:, k1:k1 + 1], -turn_ref[:, RADIX + k1:RADIX + k1 + 1]
                )
            for part in range(2):
                field[part, k1 * short:(k1 + 1) * short, :] = pair[part]
    for start in range(0, short, SUB):
        values = [
            tuple(
                field[part, k1 * short + start:k1 * short + start + SUB, :] for part in range(2)
            )
            for k1 in range(RADIX)
        ]
        mixed = dft8(values, 1)
        for n1 in range(RADIX):
            for part in range(2):
                field[part, n1 * short + start:n1 * short + start + SUB, :] = mixed[n1][part]
    for slab in range(slabs):
        for at in range(rows // tile):
            for part in range(2):
                begin = slab * rows + at * tile
                code, exponent = encode(field[part, begin:begin + tile, :])
                stack[slab, part * rows + at * tile:part * rows + (at + 1) * tile, :] = code
                scale[slab, 2 * at + part:2 * at + part + 1, :] = exponent
    for hop in range(slabs):
        outs[hop][:2 * rows, :] = stack[me ^ hop]
        outs[hop][2 * rows:, :] = scale[me ^ hop].astype(jnp.int32).astype(I16)
    if packs:
        pack_copies(
            slabs, me, source_ref, prints_ref, packed, semaphore, lambda copy: copy.wait()
        )


def finish_kernel(slabs, chunks, me_ref, gain_ref, *rest):
    ins, rest = rest[:slabs * chunks], rest[slabs * chunks:]
    lead_ref, trail_ref, turn_ref, prints_ref, index_ref, out_ref, value_ref = rest[:7]
    stack, scale, high, low, field, blocks = rest[7:]
    step, last = pl.program_id(0), pl.num_programs(0) - 1
    short = turn_ref.shape[1]
    halves, tile = short // LANES, high.shape[0] // RADIX
    rows = stack.shape[2] // 2
    width = stack.shape[3]
    stride = 2 * RADIX * halves

    @pl.when(step == 0)
    def _():
        for chunk in range(chunks):
            for hop in range(slabs):
                slab = me_ref[0] ^ hop
                stack[chunk, slab] = ins[chunk * slabs + hop][:2 * rows, :]
                scale[chunk, slab] = scales(ins[chunk * slabs + hop][2 * rows:, :])

    own = short * RADIX // slabs
    for slab in range(slabs):
        k1, base = slab * own // short, slab * own % short
        for chunk in range(chunks):
            for part in range(2):
                place = pl.multiple_of(part * rows + step * tile, SUB)
                value = (
                    stack[chunk, slab, pl.ds(place, tile), :].astype(jnp.int32).astype(F32)
                    * scale[chunk, slab, pl.ds(2 * step + part, 1), :]
                )
                at = part * short + base + chunk * width
                one, two = split(value)
                high[k1 * tile:(k1 + 1) * tile, at:at + width] = one
                low[k1 * tile:(k1 + 1) * tile, at:at + width] = two
    mixed = (
        dot(high[...], lead_ref[...]) + dot(low[...], lead_ref[...]) + dot(high[...], trail_ref[...])
    )
    gain = gain_ref[0]
    for start in range(0, tile, SUB):
        for half in range(halves):
            lanes = slice(half * LANES, (half + 1) * LANES)
            values = []
            for k1 in range(RADIX):
                place = slice(k1 * tile + start, k1 * tile + start + SUB)
                at = half * LANES
                pair = (mixed[place, at:at + LANES], mixed[place, short + at:short + at + LANES])
                if k1:
                    pair = spin(
                        pair, turn_ref[k1:k1 + 1, lanes], -turn_ref[RADIX + k1:RADIX + k1 + 1, lanes]
                    )
                values.append(pair)
            done = dft8(values, 1)
            for n1 in range(RADIX):
                column = n1 * halves + half
                for part in range(2):
                    value = done[n1][part] * gain
                    out_ref[pl.ds(start * stride + column * 2 + part, SUB, stride=stride), :] = value
                    place = pl.multiple_of(step * tile + start, SUB)
                    field[part * RADIX * halves + column, pl.ds(place, SUB), :] = value

    @pl.when(step == last)
    def _():
        band_rows = prints_ref.shape[0] // LANES
        bands = field.shape[1] // band_rows
        count = field.shape[0]
        for column in range(count):
            for row in range(band_rows):
                piece = field[column, pl.ds(row, bands, stride=band_rows), :]
                blocks[column * bands:(column + 1) * bands, row * LANES:(row + 1) * LANES] = (
                    piece.astype(BF16)
                )
        values = dot(blocks[...], prints_ref[...])
        each = count // 2 * bands
        chosen = lax.broadcasted_iota(jnp.int32, (each, 1), 0) == index_ref[...]
        tiles = index_ref.shape[1] // LANES
        for part in range(2):
            line = jnp.sum(
                jnp.where(chosen, values[part * each:(part + 1) * each, :], 0.0), axis=0, keepdims=True
            )
            for at in range(tiles):
                value_ref[0, part * tiles + at:part * tiles + at + 1, :] = (
                    line[:, at * LANES:(at + 1) * LANES]
                )
        for copy in range(1, value_ref.shape[0]):
            value_ref[copy] = value_ref[0]


def small_kernel(
    slabs, lanes_q, each, total, row_ref, lane_ref, all_ref, pick_ref, sketch_ref, factor_ref, basis_ref,
    own, found,
):
    probes = lanes_q * each
    tiles = all_ref.shape[1] // each
    gram = {}
    for one in range(probes):
        for two in range(one + 1):
            sum_here = None
            for slab in range(slabs):
                left = all_ref[slab * lanes_q + one // each, (one % each) * tiles:(one % each + 1) * tiles, :]
                right = all_ref[slab * lanes_q + two // each, (two % each) * tiles:(two % each + 1) * tiles, :]
                term = left * right
                sum_here = term if sum_here is None else sum_here + term
            sum_here = jnp.sum(jnp.sum(sum_here, axis=0, keepdims=True), axis=1, keepdims=True)
            gram[one, two] = sum_here * (1.0 / total)
    lower, inverse = {}, {}
    for at in range(probes):
        left = gram[at, at]
        for back in range(at):
            left = left - lower[at, back] * lower[at, back]
        root = jnp.sqrt(left)
        lower[at, at] = root
        inverse[at] = 1.0 / root
        for down in range(at + 1, probes):
            value = gram[down, at]
            for back in range(at):
                value = value - lower[down, back] * lower[at, back]
            lower[down, at] = value * inverse[at]
    row = lax.broadcasted_iota(jnp.int32, (probes, probes), 0)
    column = lax.broadcasted_iota(jnp.int32, (probes, probes), 1)
    factor = jnp.zeros((probes, probes), F32)
    for one in range(probes):
        for two in range(one + 1):
            factor = jnp.where((row == two) & (column == one), lower[one, two], factor)
    factor_ref[...] = factor
    for slab in range(slabs):
        for one in range(probes):
            own[one:one + 1, slab * LANES:(slab + 1) * LANES] = all_ref[
                slab * lanes_q + one // each, pl.ds((one % each) * tiles + row_ref[slab], 1), :
            ]
    value = own[...]
    first = value.astype(BF16)
    rest = value - first.astype(F32)
    second = rest.astype(BF16)
    third = (rest - second.astype(F32)).astype(BF16)
    sketch = dot(first, pick_ref[...]) + dot(second, pick_ref[...]) + dot(third, pick_ref[...])
    found[0] = sketch
    solved = []
    for at in range(probes):
        value = sketch[at:at + 1, :]
        for back in range(at):
            value = value - lower[at, back] * solved[back]
        solved.append(value * inverse[at])
        found[1, at:at + 1, :] = solved[at]
    for part in range(each):
        place = pl.ds(lane_ref[0] * each + part, 1)
        sketch_ref[part:part + 1, :] = found[0, place, :]
        basis_ref[part:part + 1, :] = found[1, place, :]


def vmem():
    return pl.BlockSpec(memory_space=pltpu.VMEM)


def smem():
    return pl.BlockSpec(memory_space=pltpu.SMEM)


def params():
    return pltpu.CompilerParams(vmem_limit_bytes=56 << 20)


def filter_power(corr_lengths, height, width):
    wave_y = jnp.arange(height // 2 + 1, dtype=jnp.int32)
    wave_x = jnp.arange(width // 2 + 1, dtype=jnp.int32)
    weight_y = jnp.where((wave_y == 0) | (wave_y == height // 2), 1.0, 2.0)
    weight_x = jnp.where((wave_x == 0) | (wave_x == width // 2), 1.0, 2.0)
    down = (corr_lengths[0] * (wave_y.astype(F32) * (2.0 * math.pi / height))) ** 2
    across = (corr_lengths[1] * (wave_x.astype(F32) * (2.0 * math.pi / width))) ** 2
    root = lax.rsqrt(1.0 + down[:, None] + across[None, :])
    return jnp.sum(root * root * root * (weight_y[:, None] * weight_x[None, :]))


def exchange(blocks, sent):
    slabs = len(blocks)
    order = sorted(range(1, slabs), key=lambda hop: (-(hop * 2 // slabs), -(hop * 4 // slabs % 2)))
    arrived = [blocks[0]] + [None] * (slabs - 1)
    for hop in order:
        pairs = [(source, source ^ hop) for source in range(slabs)]
        block = blocks[hop]
        if len(sent) >= WINDOW:
            block, _ = lax.optimization_barrier((block, sent[-WINDOW]))
        arrived[hop] = lax.ppermute(block, "grid", pairs)
        sent.append(arrived[hop])
    return arrived


def local(probes, corr_lengths, footprints, reading_slab, reading_band, reading_tile):
    rows, each, width = probes.shape
    slabs, lanes_q = lax.axis_size("grid"), lax.axis_size("probe")
    me, lane_at = lax.axis_index("grid"), lax.axis_index("probe")
    height = rows * slabs
    short = width // RADIX
    own = width // slabs
    cut = min(LANES, own)
    chunks = own // cut
    tile = min(TILE, rows)
    halves = short // LANES
    lead, trail, back_lead, back_trail = (jnp.asarray(part) for part in dft_blocks(short))
    turn_x = jnp.asarray(twiddles(width))
    turn_y = jnp.asarray(twiddles(height).T.copy())
    me_list = me.reshape(1).astype(jnp.int32)
    column_tiles = width // LANES
    flat = (
        probes.reshape(rows, each, column_tiles, LANES)
        .transpose(0, 2, 1, 3)
        .reshape(rows * each * column_tiles, LANES)
    )
    payload = jax.ShapeDtypeStruct((2 * rows + RADIX, cut), I16)

    def whole(shape):
        return pl.BlockSpec(shape, lambda step: (0,) * len(shape))

    sent = pl.pallas_call(
        lambda *refs: rows_kernel(slabs, chunks, *refs),
        grid=(rows // tile,),
        in_specs=[
            smem(),
            pl.BlockSpec((tile * each * column_tiles, LANES), lambda step: (step, 0)),
            whole(lead.shape),
            whole(trail.shape),
            whole(turn_x.shape),
        ],
        out_specs=[whole(payload.shape)] * (chunks * slabs),
        out_shape=[payload] * (chunks * slabs),
        scratch_shapes=[
            pltpu.VMEM((chunks, slabs, 2 * rows, cut), I16),
            pltpu.VMEM((chunks, slabs, RADIX, cut), F32),
            pltpu.VMEM((RADIX * tile, 2 * short), BF16),
            pltpu.VMEM((RADIX * tile, 2 * short), BF16),
        ],
        compiler_params=params(),
        name="rows_forward",
    )(me_list, flat, lead, trail, turn_x)

    history = []
    arrived = []
    for chunk in range(chunks):
        arrived.append(exchange(sent[chunk * slabs:(chunk + 1) * slabs], history))

    read_count, band_rows, tile_cols = footprints.shape
    band_count = rows // band_rows
    tile_count = width // tile_cols
    capacity = 2 * read_count // slabs
    share = capacity // lanes_q
    slots = slabs * capacity
    target, _ = lax.optimization_barrier((reading_slab[:, 0], history[slabs // 2]))
    reading = jnp.arange(read_count, dtype=jnp.int32)
    onehot = (target[:, None] == jnp.arange(slabs, dtype=jnp.int32)[None, :]).astype(F32)
    before = (reading[:, None] > reading[None, :]).astype(F32)
    slot = jnp.sum(jnp.dot(before, onehot) * onehot, axis=1).astype(jnp.int32)
    place = target * capacity + slot
    blocks = band_count * tile_count
    code = reading_tile * band_count + reading_band
    wanted = (
        jnp.arange(slabs, dtype=jnp.int32)[:, None] * capacity
        + lane_at * share
        + jnp.arange(share, dtype=jnp.int32)[None, :]
    ).reshape(-1)
    found = jnp.max(
        jnp.where(wanted[:, None] == place[None, :], (reading * blocks + code)[None, :], -1), axis=1
    )
    source = jnp.where(found < 0, -1, found // blocks)
    codes = jnp.where(found < 0, 0, found % blocks).astype(BF16).reshape(slabs, 1, share)
    codes = jnp.pad(codes, ((0, 0), (0, band_rows - 1), (0, tile_cols - share)))

    halfway = []
    group = 256 // cut if cut % LANES == 0 else 1
    parcel = jax.ShapeDtypeStruct((share + 1, band_rows, tile_cols), BF16)
    for chunk in range(chunks):
        packs = chunk == 0
        results = pl.pallas_call(
            lambda *refs, chunk=chunk, packs=packs: columns_kernel(slabs, chunk, height, packs, *refs),
            in_specs=[smem(), smem()]
            + ([smem(), pl.BlockSpec(memory_space=pl.ANY), vmem()] if packs else [])
            + [vmem()] * (slabs + 5),
            out_specs=[vmem()] * (2 * slabs if packs else slabs),
            out_shape=[payload] * slabs + ([parcel] * slabs if packs else []),
            scratch_shapes=([pltpu.SemaphoreType.DMA] if packs else [])
            + [
                pltpu.VMEM((slabs, 2 * rows, cut), I16),
                pltpu.VMEM((slabs, RADIX, cut), F32),
                pltpu.VMEM((2, height, cut), F32),
                pltpu.VMEM((RADIX // group, 2 * short, group * cut), BF16),
                pltpu.VMEM((RADIX // group, 2 * short, group * cut), BF16),
            ],
            compiler_params=params(),
            name="columns",
        )(
            me_list,
            corr_lengths,
            *([source, footprints, codes] if packs else []),
            *arrived[chunk],
            lead,
            trail,
            back_lead,
            back_trail,
            turn_y,
        )
        halfway.append(list(results[:slabs]))
        if packs:
            parcels = results[slabs:]

    shared = jnp.stack(exchange(parcels, history))
    gathered = lax.all_gather(shared, "probe", axis=0, tiled=False)
    prints = gathered[:, :, :share].transpose(3, 4, 1, 0, 2).reshape(band_rows * tile_cols, slots)
    index = gathered[:, :, share, 0, :share].transpose(1, 0, 2).reshape(1, slots).astype(jnp.int32)

    gain = lax.rsqrt(filter_power(corr_lengths, height, width) / (height * width)) / (height * width)

    returned = []
    for results in halfway:
        returned += exchange(results, history)

    group_count = slabs * lanes_q
    smoothed, values = pl.pallas_call(
        lambda *refs: finish_kernel(slabs, chunks, *refs),
        grid=(rows // tile,),
        in_specs=[smem(), smem()]
        + [whole(payload.shape)] * (chunks * slabs)
        + [
            whole(lead.shape),
            whole(trail.shape),
            whole(turn_x.shape),
            whole(prints.shape),
            whole(index.shape),
        ],
        out_specs=[
            pl.BlockSpec((tile * each * column_tiles, LANES), lambda step: (step, 0)),
            whole((group_count, each * slots // LANES, LANES)),
        ],
        out_shape=[
            jax.ShapeDtypeStruct(flat.shape, F32),
            jax.ShapeDtypeStruct((group_count, each * slots // LANES, LANES), F32),
        ],
        scratch_shapes=[
            pltpu.VMEM((chunks, slabs, 2 * rows, cut), I16),
            pltpu.VMEM((chunks, slabs, RADIX, cut), F32),
            pltpu.VMEM((RADIX * tile, 2 * short), BF16),
            pltpu.VMEM((RADIX * tile, 2 * short), BF16),
            pltpu.VMEM((each * column_tiles, rows, LANES), F32),
            pltpu.VMEM((each * column_tiles * band_count, band_rows * tile_cols), BF16),
        ],
        compiler_params=params(),
        name="rows_back",
    )(me_list, gain.reshape(1), *returned, back_lead, back_trail, turn_x, prints, index)
    smoothed = (
        smoothed.reshape(rows, column_tiles, each, LANES).transpose(0, 2, 1, 3).reshape(rows, each, width)
    )

    everyone = lax.all_to_all(values, ("grid", "probe"), split_axis=0, concat_axis=0, tiled=True)
    offset = (me ^ jnp.arange(slabs, dtype=jnp.int32)) * capacity
    lane_of = target * LANES + (me ^ target) * capacity % LANES + slot
    pick = (jnp.arange(slabs * LANES, dtype=jnp.int32)[:, None] == lane_of[None, :]).astype(BF16)
    probe_count = each * lanes_q
    sketch, factor, basis = pl.pallas_call(
        lambda *refs: small_kernel(slabs, lanes_q, each, read_count * slabs, *refs),
        in_specs=[smem(), smem(), vmem(), vmem()],
        out_specs=[vmem()] * 3,
        out_shape=[
            jax.ShapeDtypeStruct((each, read_count), F32),
            jax.ShapeDtypeStruct((probe_count, probe_count), F32),
            jax.ShapeDtypeStruct((each, read_count), F32),
        ],
        scratch_shapes=[
            pltpu.VMEM((probe_count, slabs * LANES), F32),
            pltpu.VMEM((2, probe_count, read_count), F32),
        ],
        compiler_params=params(),
        name="factor_basis",
    )(offset // LANES, lane_at.reshape(1).astype(jnp.int32), everyone, pick)
    return (smoothed, sketch.T, factor, basis.T)


def solution(mesh):
    in_specs = (
        P("grid", "probe", None),
        P(),
        P("grid", None, None),
        P("grid", None),
        P("grid"),
        P("grid"),
    )
    out_specs = (P("grid", "probe", None), P("grid", "probe"), P(), P("grid", "probe"))
    return jax.shard_map(local, mesh=mesh, in_specs=in_specs, out_specs=out_specs, check_vma=False)
```

```python
import math

import jax
import jax.numpy as jnp
import ml_dtypes
import numpy as np
from jax import lax
from jax.experimental import pallas as pl
from jax.experimental.pallas import tpu as pltpu
from jax.sharding import PartitionSpec as P

RADIX = 8
STEPS = 64.0
TOP = 32700.0
TILE = 64
SUB = 16
LANES = 128
WINDOW = 5
F32 = jnp.float32
BF16 = jnp.bfloat16
I16 = jnp.int16


def dft_blocks(length):
    grid = np.outer(np.arange(length), np.arange(length)) % length
    cosine, sine = np.cos(2 * np.pi * grid / length), np.sin(2 * np.pi * grid / length)
    forward = np.block([[cosine, -sine], [sine, cosine]]).astype(np.float32)
    lead = forward.astype(ml_dtypes.bfloat16)
    trail = (forward - lead.astype(np.float32)).astype(ml_dtypes.bfloat16)
    return lead, trail, lead.T.copy(), trail.T.copy()


def twiddles(length):
    short = length // RADIX
    angle = 2 * np.pi * np.outer(np.arange(RADIX), np.arange(short)) / length
    return np.concatenate([np.cos(angle), -np.sin(angle)]).astype(np.float32)


def turn(pair, sign):
    return (pair[1], -pair[0]) if sign < 0 else (-pair[1], pair[0])


def add(one, two):
    return (one[0] + two[0], one[1] + two[1])


def sub(one, two):
    return (one[0] - two[0], one[1] - two[1])


def dft8(x, sign):
    half = math.sqrt(0.5)
    a0, a1 = add(x[0], x[4]), sub(x[0], x[4])
    a2, a3 = add(x[2], x[6]), turn(sub(x[2], x[6]), sign)
    b0, b1 = add(x[1], x[5]), sub(x[1], x[5])
    b2, b3 = add(x[3], x[7]), turn(sub(x[3], x[7]), sign)
    even, odd = add(a0, a2), add(b0, b2)
    side, cross = sub(a0, a2), turn(sub(b0, b2), sign)
    c1, d1 = add(a1, a3), add(b1, b3)
    c3, d3 = sub(a1, a3), sub(b1, b3)
    t1, t3 = turn(d1, sign), turn(d3, sign)
    w1 = (half * (d1[0] + t1[0]), half * (d1[1] + t1[1]))
    w3 = (half * (t3[0] - d3[0]), half * (t3[1] - d3[1]))
    return [
        add(even, odd), add(c1, w1), add(side, cross), add(c3, w3),
        sub(even, odd), sub(c1, w1), sub(side, cross), sub(c3, w3),
    ]


def spin(pair, cosine, sine):
    return (pair[0] * cosine - pair[1] * sine, pair[0] * sine + pair[1] * cosine)


def split(value):
    lead = value.astype(BF16)
    return lead, (value - lead.astype(F32)).astype(BF16)


def dot(one, two):
    return jnp.dot(one, two, preferred_element_type=F32)


def encode(value):
    top = jnp.maximum(jnp.max(jnp.abs(value), axis=0, keepdims=True), 1e-30)
    exponent = jnp.ceil(jnp.log2(top) * STEPS)
    code = jnp.round(value * (jnp.exp2(exponent * (-1.0 / STEPS)) * TOP))
    return code.astype(jnp.int32).astype(I16), exponent


def scales(exponent):
    return jnp.exp2(exponent.astype(jnp.int32).astype(F32) * (1.0 / STEPS)) * (1.0 / TOP)


def pack_kernel(source_ref, prints_ref, code_ref, packed, semaphore):
    slabs, share = packed.shape[0], packed.shape[1] - 1

    def begin(at, carry):
        for slab in range(slabs):
            pltpu.make_async_copy(
                prints_ref.at[source_ref[slab * share + at]], packed.at[slab, at], semaphore
            ).start()
        return carry

    lax.fori_loop(0, share, begin, 0)
    codes = jnp.broadcast_to(code_ref[...], packed.shape[2:]).astype(BF16)
    for slab in range(slabs):
        packed[slab, share] = codes
    pltpu.make_async_copy(
        packed.at[:, pl.ds(0, share)], packed.at[:, pl.ds(0, share)], semaphore
    ).wait()


def rows_kernel(slabs, chunks, me_ref, x_ref, lead_ref, trail_ref, turn_ref, *rest):
    outs, (stack, marks, high, low) = rest[: slabs * chunks], rest[slabs * chunks:]
    step, last = pl.program_id(0), pl.num_programs(0) - 1
    short = turn_ref.shape[1]
    halves, tile = short // LANES, high.shape[0] // RADIX
    rows = (outs[0].shape[0] - RADIX) // 2
    width = outs[0].shape[1]
    stride = 2 * RADIX * halves
    for start in range(0, tile, SUB):
        for half in range(halves):
            values = []
            for n1 in range(RADIX):
                at = start * stride + (n1 * halves + half) * 2
                values.append(
                    tuple(x_ref[pl.ds(at + part, SUB, stride=stride), :] for part in range(2))
                )
            mixed = dft8(values, -1)
            for k1 in range(RADIX):
                lanes = slice(half * LANES, (half + 1) * LANES)
                pair = mixed[k1]
                if k1:
                    pair = spin(
                        pair, turn_ref[k1:k1 + 1, lanes], turn_ref[RADIX + k1:RADIX + k1 + 1, lanes]
                    )
                for part in range(2):
                    at = part * short + half * LANES
                    lead, trail = split(pair[part])
                    high[k1 * tile + start:k1 * tile + start + SUB, at:at + LANES] = lead
                    low[k1 * tile + start:k1 * tile + start + SUB, at:at + LANES] = trail
    spectrum = (
        dot(high[...], lead_ref[...]) + dot(low[...], lead_ref[...]) + dot(high[...], trail_ref[...])
    )
    own = short * RADIX // slabs
    for slab in range(slabs):
        k1, base = slab * own // short, slab * own % short
        for chunk in range(chunks):
            for part in range(2):
                at = part * short + base + chunk * width
                code, exponent = encode(
                    spectrum[k1 * tile:(k1 + 1) * tile, at:at + width]
                )
                place = pl.multiple_of(part * rows + step * tile, SUB)
                stack[chunk, slab, pl.ds(place, tile), :] = code
                marks[chunk, slab, pl.ds(2 * step + part, 1), :] = exponent

    @pl.when(step == last)
    def _():
        for chunk in range(chunks):
            for hop in range(slabs):
                slab = me_ref[0] ^ hop
                out = outs[chunk * slabs + hop]
                out[:2 * rows, :] = stack[chunk, slab]
                out[2 * rows:, :] = marks[chunk, slab].astype(jnp.int32).astype(I16)


def columns_kernel(slabs, chunk, length, me_ref, corr_ref, *rest):
    me = me_ref[0]
    ins, rest = rest[:slabs], rest[slabs:]
    back_lead, back_trail, lead, trail, turn_ref = rest[:5]
    outs, (stack, scale, field, high, low) = rest[5:5 + slabs], rest[5 + slabs:]
    short = length // RADIX
    rows = stack.shape[1] // 2
    width = stack.shape[2]
    tile = min(TILE, rows)
    group = high.shape[2] // width
    for hop in range(slabs):
        stack[me ^ hop] = ins[hop][:2 * rows, :]
        scale[me ^ hop] = scales(ins[hop][2 * rows:, :])
    for start in range(0, short, SUB):
        values = []
        for n1 in range(RADIX):
            slab, row = divmod(n1 * short + start, rows)
            mark = 2 * (row // tile)
            values.append(
                tuple(
                    stack[slab, part * rows + row:part * rows + row + SUB, :].astype(jnp.int32).astype(F32)
                    * scale[slab, mark + part:mark + part + 1, :]
                    for part in range(2)
                )
            )
        mixed = dft8(values, -1)
        for k1 in range(RADIX):
            pair = mixed[k1]
            if k1:
                pair = spin(
                    pair,
                    turn_ref[start:start + SUB, k1:k1 + 1],
                    turn_ref[start:start + SUB, RADIX + k1:RADIX + k1 + 1],
                )
            at = (k1 % group) * width
            for part in range(2):
                one, two = split(pair[part])
                place = slice(part * short + start, part * short + start + SUB)
                high[k1 // group, place, at:at + width] = one
                low[k1 // group, place, at:at + width] = two
    place = me * (length // slabs) + chunk * width
    lane = place + lax.broadcasted_iota(jnp.int32, (1, width), 1)
    wave_x = (lane // short) + RADIX * (lane % short)
    wave_x = jnp.where(wave_x < length // 2, wave_x, wave_x - length).astype(F32)
    unit = 2.0 * math.pi / length
    across = (corr_ref[1] * (wave_x * unit)) ** 2 + 1.0
    count = lax.broadcasted_iota(jnp.int32, (short, 1), 0)
    for pair_at in range(RADIX // group):
        one, two = high[pair_at], low[pair_at]
        spectrum = dot(lead[...], one) + dot(lead[...], two) + dot(trail[...], one)
        for slot in range(group):
            k1 = pair_at * group + slot
            wave_y = k1 + RADIX * count
            wave_y = jnp.where(wave_y < length // 2, wave_y, wave_y - length).astype(F32)
            down = (corr_ref[0] * (wave_y * unit)) ** 2
            root = lax.rsqrt(down + across)
            shape = root * root * lax.rsqrt(root)
            lanes = slice(slot * width, (slot + 1) * width)
            for part in range(2):
                place = slice(part * short, (part + 1) * short)
                one, two = split(spectrum[place, lanes] * shape)
                high[pair_at, place, lanes] = one
                low[pair_at, place, lanes] = two
        one, two = high[pair_at], low[pair_at]
        spectrum = (
            dot(back_lead[...], one) + dot(back_lead[...], two) + dot(back_trail[...], one)
        )
        for slot in range(group):
            k1 = pair_at * group + slot
            lanes = slice(slot * width, (slot + 1) * width)
            pair = (spectrum[:short, lanes], spectrum[short:, lanes])
            if k1:
                pair = spin(
                    pair, turn_ref[:, k1:k1 + 1], -turn_ref[:, RADIX + k1:RADIX + k1 + 1]
                )
            for part in range(2):
                field[part, k1 * short:(k1 + 1) * short, :] = pair[part]
    for start in range(0, short, SUB):
        values = [
            tuple(
                field[part, k1 * short + start:k1 * short + start + SUB, :] for part in range(2)
            )
            for k1 in range(RADIX)
        ]
        mixed = dft8(values, 1)
        for n1 in range(RADIX):
            for part in range(2):
                field[part, n1 * short + start:n1 * short + start + SUB, :] = mixed[n1][part]
    for slab in range(slabs):
        for at in range(rows // tile):
            for part in range(2):
                begin = slab * rows + at * tile
                code, exponent = encode(field[part, begin:begin + tile, :])
                stack[slab, part * rows + at * tile:part * rows + (at + 1) * tile, :] = code
                scale[slab, 2 * at + part:2 * at + part + 1, :] = exponent
    for hop in range(slabs):
        outs[hop][:2 * rows, :] = stack[me ^ hop]
        outs[hop][2 * rows:, :] = scale[me ^ hop].astype(jnp.int32).astype(I16)


def finish_kernel(slabs, chunks, me_ref, gain_ref, *rest):
    ins, rest = rest[:slabs * chunks], rest[slabs * chunks:]
    lead_ref, trail_ref, turn_ref, prints_ref, index_ref, out_ref, value_ref = rest[:7]
    stack, scale, high, low, field, blocks = rest[7:]
    step, last = pl.program_id(0), pl.num_programs(0) - 1
    short = turn_ref.shape[1]
    halves, tile = short // LANES, high.shape[0] // RADIX
    rows = stack.shape[2] // 2
    width = stack.shape[3]
    stride = 2 * RADIX * halves

    @pl.when(step == 0)
    def _():
        for chunk in range(chunks):
            for hop in range(slabs):
                slab = me_ref[0] ^ hop
                stack[chunk, slab] = ins[chunk * slabs + hop][:2 * rows, :]
                scale[chunk, slab] = scales(ins[chunk * slabs + hop][2 * rows:, :])

    own = short * RADIX // slabs
    for slab in range(slabs):
        k1, base = slab * own // short, slab * own % short
        for chunk in range(chunks):
            for part in range(2):
                place = pl.multiple_of(part * rows + step * tile, SUB)
                value = (
                    stack[chunk, slab, pl.ds(place, tile), :].astype(jnp.int32).astype(F32)
                    * scale[chunk, slab, pl.ds(2 * step + part, 1), :]
                )
                at = part * short + base + chunk * width
                one, two = split(value)
                high[k1 * tile:(k1 + 1) * tile, at:at + width] = one
                low[k1 * tile:(k1 + 1) * tile, at:at + width] = two
    mixed = (
        dot(high[...], lead_ref[...]) + dot(low[...], lead_ref[...]) + dot(high[...], trail_ref[...])
    )
    gain = gain_ref[0]
    for start in range(0, tile, SUB):
        for half in range(halves):
            lanes = slice(half * LANES, (half + 1) * LANES)
            values = []
            for k1 in range(RADIX):
                place = slice(k1 * tile + start, k1 * tile + start + SUB)
                at = half * LANES
                pair = (mixed[place, at:at + LANES], mixed[place, short + at:short + at + LANES])
                if k1:
                    pair = spin(
                        pair, turn_ref[k1:k1 + 1, lanes], -turn_ref[RADIX + k1:RADIX + k1 + 1, lanes]
                    )
                values.append(pair)
            done = dft8(values, 1)
            for n1 in range(RADIX):
                column = n1 * halves + half
                for part in range(2):
                    value = done[n1][part] * gain
                    out_ref[pl.ds(start * stride + column * 2 + part, SUB, stride=stride), :] = value
                    place = pl.multiple_of(step * tile + start, SUB)
                    field[part * RADIX * halves + column, pl.ds(place, SUB), :] = value

    @pl.when(step == last)
    def _():
        band_rows = prints_ref.shape[0] // LANES
        bands = field.shape[1] // band_rows
        count = field.shape[0]
        for column in range(count):
            for row in range(band_rows):
                piece = field[column, pl.ds(row, bands, stride=band_rows), :]
                blocks[column * bands:(column + 1) * bands, row * LANES:(row + 1) * LANES] = (
                    piece.astype(BF16)
                )
        values = dot(blocks[...], prints_ref[...])
        each = count // 2 * bands
        chosen = lax.broadcasted_iota(jnp.int32, (each, 1), 0) == index_ref[...]
        tiles = index_ref.shape[1] // LANES
        for part in range(2):
            line = jnp.sum(
                jnp.where(chosen, values[part * each:(part + 1) * each, :], 0.0), axis=0, keepdims=True
            )
            for at in range(tiles):
                value_ref[0, part * tiles + at:part * tiles + at + 1, :] = (
                    line[:, at * LANES:(at + 1) * LANES]
                )
        for copy in range(1, value_ref.shape[0]):
            value_ref[copy] = value_ref[0]


def small_kernel(
    slabs, lanes_q, each, total, row_ref, lane_ref, all_ref, pick_ref, sketch_ref, factor_ref, basis_ref,
    own, found,
):
    probes = lanes_q * each
    tiles = all_ref.shape[1] // each
    gram = {}
    for one in range(probes):
        for two in range(one + 1):
            sum_here = None
            for slab in range(slabs):
                left = all_ref[slab * lanes_q + one // each, (one % each) * tiles:(one % each + 1) * tiles, :]
                right = all_ref[slab * lanes_q + two // each, (two % each) * tiles:(two % each + 1) * tiles, :]
                term = left * right
                sum_here = term if sum_here is None else sum_here + term
            sum_here = jnp.sum(jnp.sum(sum_here, axis=0, keepdims=True), axis=1, keepdims=True)
            gram[one, two] = sum_here * (1.0 / total)
    lower, inverse = {}, {}
    for at in range(probes):
        left = gram[at, at]
        for back in range(at):
            left = left - lower[at, back] * lower[at, back]
        root = jnp.sqrt(left)
        lower[at, at] = root
        inverse[at] = 1.0 / root
        for down in range(at + 1, probes):
            value = gram[down, at]
            for back in range(at):
                value = value - lower[down, back] * lower[at, back]
            lower[down, at] = value * inverse[at]
    row = lax.broadcasted_iota(jnp.int32, (probes, probes), 0)
    column = lax.broadcasted_iota(jnp.int32, (probes, probes), 1)
    factor = jnp.zeros((probes, probes), F32)
    for one in range(probes):
        for two in range(one + 1):
            factor = jnp.where((row == two) & (column == one), lower[one, two], factor)
    factor_ref[...] = factor
    for slab in range(slabs):
        for one in range(probes):
            own[one:one + 1, slab * LANES:(slab + 1) * LANES] = all_ref[
                slab * lanes_q + one // each, pl.ds((one % each) * tiles + row_ref[slab], 1), :
            ]
    value = own[...]
    first = value.astype(BF16)
    rest = value - first.astype(F32)
    second = rest.astype(BF16)
    third = (rest - second.astype(F32)).astype(BF16)
    sketch = dot(first, pick_ref[...]) + dot(second, pick_ref[...]) + dot(third, pick_ref[...])
    found[0] = sketch
    solved = []
    for at in range(probes):
        value = sketch[at:at + 1, :]
        for back in range(at):
            value = value - lower[at, back] * solved[back]
        solved.append(value * inverse[at])
        found[1, at:at + 1, :] = solved[at]
    for part in range(each):
        place = pl.ds(lane_ref[0] * each + part, 1)
        sketch_ref[part:part + 1, :] = found[0, place, :]
        basis_ref[part:part + 1, :] = found[1, place, :]


def vmem():
    return pl.BlockSpec(memory_space=pltpu.VMEM)


def smem():
    return pl.BlockSpec(memory_space=pltpu.SMEM)


def params():
    return pltpu.CompilerParams(vmem_limit_bytes=56 << 20)


def filter_power(corr_lengths, height, width):
    wave_y = jnp.arange(height // 2 + 1, dtype=jnp.int32)
    wave_x = jnp.arange(width // 2 + 1, dtype=jnp.int32)
    weight_y = jnp.where((wave_y == 0) | (wave_y == height // 2), 1.0, 2.0)
    weight_x = jnp.where((wave_x == 0) | (wave_x == width // 2), 1.0, 2.0)
    down = (corr_lengths[0] * (wave_y.astype(F32) * (2.0 * math.pi / height))) ** 2
    across = (corr_lengths[1] * (wave_x.astype(F32) * (2.0 * math.pi / width))) ** 2
    root = lax.rsqrt(1.0 + down[:, None] + across[None, :])
    return jnp.sum(root * root * root * (weight_y[:, None] * weight_x[None, :]))


def send(value, axis, hop, sent):
    pairs = [(source, source ^ hop) for source in range(lax.axis_size(axis))]
    if len(sent) >= WINDOW:
        value, _ = lax.optimization_barrier((value, sent[-WINDOW]))
    return lax.ppermute(value, axis, pairs)


def exchange(blocks, sent):
    slabs = len(blocks)
    far, near = range(slabs - 1, slabs // 2 - 1, -1), range(slabs // 2 - 1, 0, -1)
    arrived = list(blocks)
    for hop in [hop for pair in zip(far, near) for hop in pair] + [far[-1]]:
        arrived[hop] = send(blocks[hop], "grid", hop, sent)
        sent.append(arrived[hop])
    return arrived


def local(probes, corr_lengths, footprints, reading_slab, reading_band, reading_tile):
    rows, each, width = probes.shape
    slabs, lanes_q = lax.axis_size("grid"), lax.axis_size("probe")
    me, lane_at = lax.axis_index("grid"), lax.axis_index("probe")
    height = rows * slabs
    short = width // RADIX
    own = width // slabs
    cut = min(LANES, own)
    chunks = own // cut
    tile = min(TILE, rows)
    halves = short // LANES
    lead, trail, back_lead, back_trail = (jnp.asarray(part) for part in dft_blocks(short))
    turn_x = jnp.asarray(twiddles(width))
    turn_y = jnp.asarray(twiddles(height).T.copy())
    me_list = me.reshape(1).astype(jnp.int32)
    read_count, band_rows, tile_cols = footprints.shape
    band_count = rows // band_rows
    tile_count = width // tile_cols
    capacity = 2 * read_count // slabs
    share = capacity // lanes_q
    slots = slabs * capacity
    target = reading_slab[:, 0]
    reading = jnp.arange(read_count, dtype=jnp.int32)
    onehot = (target[:, None] == jnp.arange(slabs, dtype=jnp.int32)[None, :]).astype(F32)
    before = (reading[:, None] > reading[None, :]).astype(F32)
    slot = jnp.sum(jnp.dot(before, onehot) * onehot, axis=1).astype(jnp.int32)
    place = target * capacity + slot
    blocks = band_count * tile_count
    code = reading_tile * band_count + reading_band
    wanted = (
        jnp.arange(slabs, dtype=jnp.int32)[:, None] * capacity
        + lane_at * share
        + jnp.arange(share, dtype=jnp.int32)[None, :]
    ).reshape(-1)
    found = jnp.max(
        jnp.where(wanted[:, None] == place[None, :], (reading * blocks + code)[None, :], -1), axis=1
    )
    source = jnp.maximum(found, 0) // blocks
    codes = jnp.where(found < 0, -1, found % blocks).astype(F32).reshape(1, slabs * share)

    packed = pl.pallas_call(
        pack_kernel,
        in_specs=[smem(), pl.BlockSpec(memory_space=pl.ANY), vmem()],
        out_specs=vmem(),
        out_shape=jax.ShapeDtypeStruct((slabs, share + 1, band_rows, tile_cols), BF16),
        scratch_shapes=[pltpu.SemaphoreType.DMA],
        compiler_params=params(),
        name="pack_prints",
    )(source, footprints, codes)
    gathered = lax.all_to_all(packed, "grid", split_axis=0, concat_axis=0, tiled=True)
    me_list, _ = lax.optimization_barrier((me_list, packed))
    column_tiles = width // LANES
    flat = (
        probes.reshape(rows, each, column_tiles, LANES)
        .transpose(0, 2, 1, 3)
        .reshape(rows * each * column_tiles, LANES)
    )
    payload = jax.ShapeDtypeStruct((2 * rows + RADIX, cut), I16)

    def whole(shape):
        return pl.BlockSpec(shape, lambda step: (0,) * len(shape))

    sent = pl.pallas_call(
        lambda *refs: rows_kernel(slabs, chunks, *refs),
        grid=(rows // tile,),
        in_specs=[
            smem(),
            pl.BlockSpec((tile * each * column_tiles, LANES), lambda step: (step, 0)),
            whole(lead.shape),
            whole(trail.shape),
            whole(turn_x.shape),
        ],
        out_specs=[whole(payload.shape)] * (chunks * slabs),
        out_shape=[payload] * (chunks * slabs),
        scratch_shapes=[
            pltpu.VMEM((chunks, slabs, 2 * rows, cut), I16),
            pltpu.VMEM((chunks, slabs, RADIX, cut), F32),
            pltpu.VMEM((RADIX * tile, 2 * short), BF16),
            pltpu.VMEM((RADIX * tile, 2 * short), BF16),
        ],
        compiler_params=params(),
        name="rows_forward",
    )(me_list, flat, lead, trail, turn_x)

    gathered, _ = lax.optimization_barrier((gathered, sent[0]))
    gathered = lax.all_gather(gathered, "probe", axis=0, tiled=False)
    history = []
    arrived = []
    for chunk in range(chunks):
        arrived.append(exchange(sent[chunk * slabs:(chunk + 1) * slabs], history))

    halfway = []
    group = 256 // cut if cut % LANES == 0 else 1
    for chunk in range(chunks):
        results = pl.pallas_call(
            lambda *refs, chunk=chunk: columns_kernel(slabs, chunk, height, *refs),
            in_specs=[smem(), smem()]
            + [vmem()] * (slabs + 5),
            out_specs=[vmem()] * slabs,
            out_shape=[payload] * slabs,
            scratch_shapes=[
                pltpu.VMEM((slabs, 2 * rows, cut), I16),
                pltpu.VMEM((slabs, RADIX, cut), F32),
                pltpu.VMEM((2, height, cut), F32),
                pltpu.VMEM((RADIX // group, 2 * short, group * cut), BF16),
                pltpu.VMEM((RADIX // group, 2 * short, group * cut), BF16),
            ],
            compiler_params=params(),
            name="columns",
        )(
            me_list,
            corr_lengths,
            *arrived[chunk],
            lead,
            trail,
            back_lead,
            back_trail,
            turn_y,
        )
        halfway.append(list(results))

    gain = lax.rsqrt(filter_power(corr_lengths, height, width) / (height * width)) / (height * width)

    returned = []
    for results in halfway:
        returned += exchange(results, history)

    prints = gathered[:, :, :share].transpose(3, 4, 1, 0, 2).reshape(band_rows * tile_cols, slots)
    index = lax.dynamic_slice_in_dim(gathered[:, :, share, 0], me * share, share, 2)
    index = index.transpose(1, 0, 2).reshape(1, slots).astype(jnp.int32)

    group_count = slabs * lanes_q
    smoothed, values = pl.pallas_call(
        lambda *refs: finish_kernel(slabs, chunks, *refs),
        grid=(rows // tile,),
        in_specs=[smem(), smem()]
        + [whole(payload.shape)] * (chunks * slabs)
        + [
            whole(lead.shape),
            whole(trail.shape),
            whole(turn_x.shape),
            whole(prints.shape),
            whole(index.shape),
        ],
        out_specs=[
            pl.BlockSpec((tile * each * column_tiles, LANES), lambda step: (step, 0)),
            whole((group_count, each * slots // LANES, LANES)),
        ],
        out_shape=[
            jax.ShapeDtypeStruct(flat.shape, F32),
            jax.ShapeDtypeStruct((group_count, each * slots // LANES, LANES), F32),
        ],
        scratch_shapes=[
            pltpu.VMEM((chunks, slabs, 2 * rows, cut), I16),
            pltpu.VMEM((chunks, slabs, RADIX, cut), F32),
            pltpu.VMEM((RADIX * tile, 2 * short), BF16),
            pltpu.VMEM((RADIX * tile, 2 * short), BF16),
            pltpu.VMEM((each * column_tiles, rows, LANES), F32),
            pltpu.VMEM((each * column_tiles * band_count, band_rows * tile_cols), BF16),
        ],
        compiler_params=params(),
        name="rows_back",
    )(me_list, gain.reshape(1), *returned, back_lead, back_trail, turn_x, prints, index)
    smoothed = (
        smoothed.reshape(rows, column_tiles, each, LANES).transpose(0, 2, 1, 3).reshape(rows, each, width)
    )

    everyone = lax.all_to_all(values, ("grid", "probe"), split_axis=0, concat_axis=0, tiled=True)
    offset = jnp.full((slabs,), me * capacity, jnp.int32)
    lane_of = target * LANES + me * capacity % LANES + slot
    pick = (jnp.arange(slabs * LANES, dtype=jnp.int32)[:, None] == lane_of[None, :]).astype(BF16)
    probe_count = each * lanes_q
    sketch, factor, basis = pl.pallas_call(
        lambda *refs: small_kernel(slabs, lanes_q, each, read_count * slabs, *refs),
        in_specs=[smem(), smem(), vmem(), vmem()],
        out_specs=[vmem()] * 3,
        out_shape=[
            jax.ShapeDtypeStruct((each, read_count), F32),
            jax.ShapeDtypeStruct((probe_count, probe_count), F32),
            jax.ShapeDtypeStruct((each, read_count), F32),
        ],
        scratch_shapes=[
            pltpu.VMEM((probe_count, slabs * LANES), F32),
            pltpu.VMEM((2, probe_count, read_count), F32),
        ],
        compiler_params=params(),
        name="factor_basis",
    )(offset // LANES, lane_at.reshape(1).astype(jnp.int32), everyone, pick)
    return (smoothed, sketch.T, factor, basis.T)


def solution(mesh):
    in_specs = (
        P("grid", "probe", None),
        P(),
        P("grid", None, None),
        P("grid", None),
        P("grid"),
        P("grid"),
    )
    out_specs = (P("grid", "probe", None), P("grid", "probe"), P(), P("grid", "probe"))
    return jax.shard_map(local, mesh=mesh, in_specs=in_specs, out_specs=out_specs, check_vma=False)
```

```python
import math

import jax
import jax.numpy as jnp
import ml_dtypes
import numpy as np
from jax import lax
from jax.experimental import pallas as pl
from jax.experimental.pallas import tpu as pltpu
from jax.sharding import PartitionSpec as P

RADIX = 8
STEPS = 64.0
TOP = 32700.0
TILE = 64
SUB = 16
LANES = 128
WINDOW = 5
F32 = jnp.float32
BF16 = jnp.bfloat16
I16 = jnp.int16


def dft_blocks(length):
    grid = np.outer(np.arange(length), np.arange(length)) % length
    cosine, sine = np.cos(2 * np.pi * grid / length), np.sin(2 * np.pi * grid / length)
    forward = np.block([[cosine, -sine], [sine, cosine]]).astype(np.float32)
    lead = forward.astype(ml_dtypes.bfloat16)
    trail = (forward - lead.astype(np.float32)).astype(ml_dtypes.bfloat16)
    return lead, trail, lead.T.copy(), trail.T.copy()


def twiddles(length):
    short = length // RADIX
    angle = 2 * np.pi * np.outer(np.arange(RADIX), np.arange(short)) / length
    return np.concatenate([np.cos(angle), -np.sin(angle)]).astype(np.float32)


def turn(pair, sign):
    return (pair[1], -pair[0]) if sign < 0 else (-pair[1], pair[0])


def add(one, two):
    return (one[0] + two[0], one[1] + two[1])


def sub(one, two):
    return (one[0] - two[0], one[1] - two[1])


def dft8(x, sign):
    half = math.sqrt(0.5)
    a0, a1 = add(x[0], x[4]), sub(x[0], x[4])
    a2, a3 = add(x[2], x[6]), turn(sub(x[2], x[6]), sign)
    b0, b1 = add(x[1], x[5]), sub(x[1], x[5])
    b2, b3 = add(x[3], x[7]), turn(sub(x[3], x[7]), sign)
    even, odd = add(a0, a2), add(b0, b2)
    side, cross = sub(a0, a2), turn(sub(b0, b2), sign)
    c1, d1 = add(a1, a3), add(b1, b3)
    c3, d3 = sub(a1, a3), sub(b1, b3)
    t1, t3 = turn(d1, sign), turn(d3, sign)
    w1 = (half * (d1[0] + t1[0]), half * (d1[1] + t1[1]))
    w3 = (half * (t3[0] - d3[0]), half * (t3[1] - d3[1]))
    return [
        add(even, odd), add(c1, w1), add(side, cross), add(c3, w3),
        sub(even, odd), sub(c1, w1), sub(side, cross), sub(c3, w3),
    ]


def spin(pair, cosine, sine):
    return (pair[0] * cosine - pair[1] * sine, pair[0] * sine + pair[1] * cosine)


def split(value):
    lead = value.astype(BF16)
    return lead, (value - lead.astype(F32)).astype(BF16)


def dot(one, two):
    return jnp.dot(one, two, preferred_element_type=F32)


def encode(value):
    top = jnp.maximum(jnp.max(jnp.abs(value), axis=0, keepdims=True), 1e-30)
    exponent = jnp.ceil(jnp.log2(top) * STEPS)
    code = jnp.round(value * (jnp.exp2(exponent * (-1.0 / STEPS)) * TOP))
    return code.astype(jnp.int32).astype(I16), exponent


def scales(exponent):
    return jnp.exp2(exponent.astype(jnp.int32).astype(F32) * (1.0 / STEPS)) * (1.0 / TOP)


def pack_kernel(
    slabs, capacity, bands, spot_ref, target_ref, band_ref, tile_ref, prints_ref, packed, place_ref, wide, flat, thin
):
    count, band_rows, _ = prints_ref.shape
    share = packed.shape[1] - 1
    sent = slabs * share
    target = target_ref[...]
    mine = (lax.broadcasted_iota(jnp.int32, (slabs, 1), 0) == target).astype(F32)
    earlier = lax.broadcasted_iota(jnp.int32, (count, count), 0) < lax.broadcasted_iota(
        jnp.int32, (count, count), 1
    )
    before = dot(mine.astype(BF16), earlier.astype(F32).astype(BF16))
    slot = jnp.sum(before * mine, axis=0, keepdims=True).astype(jnp.int32)
    place = target * capacity + slot
    place_ref[...] = place
    order = lax.broadcasted_iota(jnp.int32, (sent, 1), 0)
    wanted = order // share * capacity + spot_ref[1] * share + order % share
    pick = (place == wanted).astype(F32).astype(BF16)
    code = (tile_ref[...] * bands + band_ref[...] + 1).astype(F32).astype(BF16)
    code = lax.dot_general(
        jnp.broadcast_to(code, (band_rows, count)), pick, (((1,), (1,)), ((), ())), preferred_element_type=F32
    )
    code = (code - 1.0).astype(BF16)
    wide[...] = prints_ref[...].astype(F32).reshape(count * band_rows, LANES)
    for row in range(band_rows):
        flat[:, row * LANES:(row + 1) * LANES] = wide[pl.ds(row, count, stride=band_rows), :].astype(BF16)
    picked = dot(pick, flat[...])
    for row in range(band_rows):
        thin[pl.ds(row, sent, stride=band_rows), :] = picked[:, row * LANES:(row + 1) * LANES]
    for slab in range(slabs):
        lines = thin[slab * share * band_rows:(slab + 1) * share * band_rows, :]
        packed[slab, :share] = lines.reshape(share, band_rows, LANES).astype(BF16)
        packed[slab, share] = code


def rows_kernel(slabs, chunks, me_ref, x_ref, lead_ref, trail_ref, turn_ref, *rest):
    outs, (stack, marks, high, low) = rest[: slabs * chunks], rest[slabs * chunks:]
    step, last = pl.program_id(0), pl.num_programs(0) - 1
    short = turn_ref.shape[1]
    halves, tile = short // LANES, high.shape[0] // RADIX
    rows = (outs[0].shape[0] - RADIX) // 2
    width = outs[0].shape[1]
    stride = 2 * RADIX * halves
    for start in range(0, tile, SUB):
        for half in range(halves):
            values = []
            for n1 in range(RADIX):
                at = start * stride + (n1 * halves + half) * 2
                values.append(
                    tuple(x_ref[pl.ds(at + part, SUB, stride=stride), :] for part in range(2))
                )
            mixed = dft8(values, -1)
            for k1 in range(RADIX):
                lanes = slice(half * LANES, (half + 1) * LANES)
                pair = mixed[k1]
                if k1:
                    pair = spin(
                        pair, turn_ref[k1:k1 + 1, lanes], turn_ref[RADIX + k1:RADIX + k1 + 1, lanes]
                    )
                for part in range(2):
                    at = part * short + half * LANES
                    lead, trail = split(pair[part])
                    high[k1 * tile + start:k1 * tile + start + SUB, at:at + LANES] = lead
                    low[k1 * tile + start:k1 * tile + start + SUB, at:at + LANES] = trail
    spectrum = (
        dot(high[...], lead_ref[...]) + dot(low[...], lead_ref[...]) + dot(high[...], trail_ref[...])
    )
    own = short * RADIX // slabs
    for slab in range(slabs):
        k1, base = slab * own // short, slab * own % short
        for chunk in range(chunks):
            for part in range(2):
                at = part * short + base + chunk * width
                code, exponent = encode(
                    spectrum[k1 * tile:(k1 + 1) * tile, at:at + width]
                )
                place = pl.multiple_of(part * rows + step * tile, SUB)
                stack[chunk, slab, pl.ds(place, tile), :] = code
                marks[chunk, slab, pl.ds(2 * step + part, 1), :] = exponent

    @pl.when(step == last)
    def _():
        for chunk in range(chunks):
            for hop in range(slabs):
                slab = me_ref[0] ^ hop
                out = outs[chunk * slabs + hop]
                out[:2 * rows, :] = stack[chunk, slab]
                out[2 * rows:, :] = marks[chunk, slab].astype(jnp.int32).astype(I16)


def columns_kernel(slabs, chunk, length, me_ref, corr_ref, *rest):
    me = me_ref[0]
    ins, rest = rest[:slabs], rest[slabs:]
    back_lead, back_trail, lead, trail, turn_ref = rest[:5]
    outs, (stack, scale, field, high, low) = rest[5:5 + slabs], rest[5 + slabs:]
    short = length // RADIX
    rows = stack.shape[1] // 2
    width = stack.shape[2]
    tile = min(TILE, rows)
    group = high.shape[2] // width
    for hop in range(slabs):
        stack[me ^ hop] = ins[hop][:2 * rows, :]
        scale[me ^ hop] = scales(ins[hop][2 * rows:, :])
    for start in range(0, short, SUB):
        values = []
        for n1 in range(RADIX):
            slab, row = divmod(n1 * short + start, rows)
            mark = 2 * (row // tile)
            values.append(
                tuple(
                    stack[slab, part * rows + row:part * rows + row + SUB, :].astype(jnp.int32).astype(F32)
                    * scale[slab, mark + part:mark + part + 1, :]
                    for part in range(2)
                )
            )
        mixed = dft8(values, -1)
        for k1 in range(RADIX):
            pair = mixed[k1]
            if k1:
                pair = spin(
                    pair,
                    turn_ref[start:start + SUB, k1:k1 + 1],
                    turn_ref[start:start + SUB, RADIX + k1:RADIX + k1 + 1],
                )
            at = (k1 % group) * width
            for part in range(2):
                one, two = split(pair[part])
                place = slice(part * short + start, part * short + start + SUB)
                high[k1 // group, place, at:at + width] = one
                low[k1 // group, place, at:at + width] = two
    place = me * (length // slabs) + chunk * width
    lane = place + lax.broadcasted_iota(jnp.int32, (1, width), 1)
    wave_x = (lane // short) + RADIX * (lane % short)
    wave_x = jnp.where(wave_x < length // 2, wave_x, wave_x - length).astype(F32)
    unit = 2.0 * math.pi / length
    across = (corr_ref[1] * (wave_x * unit)) ** 2 + 1.0
    count = lax.broadcasted_iota(jnp.int32, (short, 1), 0)
    for pair_at in range(RADIX // group):
        one, two = high[pair_at], low[pair_at]
        spectrum = dot(lead[...], one) + dot(lead[...], two) + dot(trail[...], one)
        for slot in range(group):
            k1 = pair_at * group + slot
            wave_y = k1 + RADIX * count
            wave_y = jnp.where(wave_y < length // 2, wave_y, wave_y - length).astype(F32)
            down = (corr_ref[0] * (wave_y * unit)) ** 2
            root = lax.rsqrt(down + across)
            shape = root * root * lax.rsqrt(root)
            lanes = slice(slot * width, (slot + 1) * width)
            for part in range(2):
                place = slice(part * short, (part + 1) * short)
                one, two = split(spectrum[place, lanes] * shape)
                high[pair_at, place, lanes] = one
                low[pair_at, place, lanes] = two
        one, two = high[pair_at], low[pair_at]
        spectrum = (
            dot(back_lead[...], one) + dot(back_lead[...], two) + dot(back_trail[...], one)
        )
        for slot in range(group):
            k1 = pair_at * group + slot
            lanes = slice(slot * width, (slot + 1) * width)
            pair = (spectrum[:short, lanes], spectrum[short:, lanes])
            if k1:
                pair = spin(
                    pair, turn_ref[:, k1:k1 + 1], -turn_ref[:, RADIX + k1:RADIX + k1 + 1]
                )
            for part in range(2):
                field[part, k1 * short:(k1 + 1) * short, :] = pair[part]
    for start in range(0, short, SUB):
        values = [
            tuple(
                field[part, k1 * short + start:k1 * short + start + SUB, :] for part in range(2)
            )
            for k1 in range(RADIX)
        ]
        mixed = dft8(values, 1)
        for n1 in range(RADIX):
            for part in range(2):
                field[part, n1 * short + start:n1 * short + start + SUB, :] = mixed[n1][part]
    for slab in range(slabs):
        for at in range(rows // tile):
            for part in range(2):
                begin = slab * rows + at * tile
                code, exponent = encode(field[part, begin:begin + tile, :])
                stack[slab, part * rows + at * tile:part * rows + (at + 1) * tile, :] = code
                scale[slab, 2 * at + part:2 * at + part + 1, :] = exponent
    for hop in range(slabs):
        outs[hop][:2 * rows, :] = stack[me ^ hop]
        outs[hop][2 * rows:, :] = scale[me ^ hop].astype(jnp.int32).astype(I16)


def finish_kernel(slabs, chunks, me_ref, gain_ref, *rest):
    ins, rest = rest[:slabs * chunks], rest[slabs * chunks:]
    lead_ref, trail_ref, turn_ref, prints_hbm, index_ref, out_ref, value_ref = rest[:7]
    stack, scale, high, low, field, blocks, prints_ref, semaphore = rest[7:]
    step, last = pl.program_id(0), pl.num_programs(0) - 1
    short = turn_ref.shape[1]
    halves, tile = short // LANES, high.shape[0] // RADIX
    rows = stack.shape[2] // 2
    width = stack.shape[3]
    stride = 2 * RADIX * halves

    @pl.when(step == 0)
    def _():
        pltpu.make_async_copy(prints_hbm, prints_ref, semaphore).start()
        for chunk in range(chunks):
            for hop in range(slabs):
                slab = me_ref[0] ^ hop
                stack[chunk, slab] = ins[chunk * slabs + hop][:2 * rows, :]
                scale[chunk, slab] = scales(ins[chunk * slabs + hop][2 * rows:, :])

    own = short * RADIX // slabs
    for slab in range(slabs):
        k1, base = slab * own // short, slab * own % short
        for chunk in range(chunks):
            for part in range(2):
                place = pl.multiple_of(part * rows + step * tile, SUB)
                value = (
                    stack[chunk, slab, pl.ds(place, tile), :].astype(jnp.int32).astype(F32)
                    * scale[chunk, slab, pl.ds(2 * step + part, 1), :]
                )
                at = part * short + base + chunk * width
                one, two = split(value)
                high[k1 * tile:(k1 + 1) * tile, at:at + width] = one
                low[k1 * tile:(k1 + 1) * tile, at:at + width] = two
    mixed = (
        dot(high[...], lead_ref[...]) + dot(low[...], lead_ref[...]) + dot(high[...], trail_ref[...])
    )
    gain = gain_ref[0]
    for start in range(0, tile, SUB):
        for half in range(halves):
            lanes = slice(half * LANES, (half + 1) * LANES)
            values = []
            for k1 in range(RADIX):
                place = slice(k1 * tile + start, k1 * tile + start + SUB)
                at = half * LANES
                pair = (mixed[place, at:at + LANES], mixed[place, short + at:short + at + LANES])
                if k1:
                    pair = spin(
                        pair, turn_ref[k1:k1 + 1, lanes], -turn_ref[RADIX + k1:RADIX + k1 + 1, lanes]
                    )
                values.append(pair)
            done = dft8(values, 1)
            for n1 in range(RADIX):
                column = n1 * halves + half
                for part in range(2):
                    value = done[n1][part] * gain
                    out_ref[pl.ds(start * stride + column * 2 + part, SUB, stride=stride), :] = value
                    place = pl.multiple_of(step * tile + start, SUB)
                    field[part * RADIX * halves + column, pl.ds(place, SUB), :] = value

    @pl.when(step == last)
    def _():
        band_rows = prints_ref.shape[0] // LANES
        bands = field.shape[1] // band_rows
        count = field.shape[0]
        for column in range(count):
            for row in range(band_rows):
                piece = field[column, pl.ds(row, bands, stride=band_rows), :]
                blocks[column * bands:(column + 1) * bands, row * LANES:(row + 1) * LANES] = (
                    piece.astype(BF16)
                )
        pltpu.make_async_copy(prints_hbm, prints_ref, semaphore).wait()
        values = dot(blocks[...], prints_ref[...])
        each = count // 2 * bands
        chosen = lax.broadcasted_iota(jnp.int32, (each, 1), 0) == index_ref[...]
        tiles = index_ref.shape[1] // LANES
        for part in range(2):
            line = jnp.sum(
                jnp.where(chosen, values[part * each:(part + 1) * each, :], 0.0), axis=0, keepdims=True
            )
            for at in range(tiles):
                value_ref[0, part * tiles + at:part * tiles + at + 1, :] = (
                    line[:, at * LANES:(at + 1) * LANES]
                )
        for copy in range(1, value_ref.shape[0]):
            value_ref[copy] = value_ref[0]


def small_kernel(
    slabs, lanes_q, each, total, capacity, spot_ref, all_ref, pick_ref, sketch_ref, factor_ref, basis_ref,
    own, found,
):
    probes = lanes_q * each
    tiles = all_ref.shape[1] // each
    gram = {}
    for one in range(probes):
        for two in range(one + 1):
            sum_here = None
            for slab in range(slabs):
                left = all_ref[slab * lanes_q + one // each, (one % each) * tiles:(one % each + 1) * tiles, :]
                right = all_ref[slab * lanes_q + two // each, (two % each) * tiles:(two % each + 1) * tiles, :]
                term = left * right
                sum_here = term if sum_here is None else sum_here + term
            sum_here = jnp.sum(jnp.sum(sum_here, axis=0, keepdims=True), axis=1, keepdims=True)
            gram[one, two] = sum_here * (1.0 / total)
    lower, inverse = {}, {}
    for at in range(probes):
        left = gram[at, at]
        for back in range(at):
            left = left - lower[at, back] * lower[at, back]
        root = jnp.sqrt(left)
        lower[at, at] = root
        inverse[at] = 1.0 / root
        for down in range(at + 1, probes):
            value = gram[down, at]
            for back in range(at):
                value = value - lower[down, back] * lower[at, back]
            lower[down, at] = value * inverse[at]
    row = lax.broadcasted_iota(jnp.int32, (probes, probes), 0)
    column = lax.broadcasted_iota(jnp.int32, (probes, probes), 1)
    factor = jnp.zeros((probes, probes), F32)
    for one in range(probes):
        for two in range(one + 1):
            factor = jnp.where((row == two) & (column == one), lower[one, two], factor)
    factor_ref[...] = factor
    for slab in range(slabs):
        for one in range(probes):
            own[one:one + 1, slab * LANES:(slab + 1) * LANES] = all_ref[
                slab * lanes_q + one // each, pl.ds((one % each) * tiles + spot_ref[0] * capacity // LANES, 1), :
            ]
    value = own[...]
    first = value.astype(BF16)
    rest = value - first.astype(F32)
    second = rest.astype(BF16)
    third = (rest - second.astype(F32)).astype(BF16)
    sketch = dot(first, pick_ref[...]) + dot(second, pick_ref[...]) + dot(third, pick_ref[...])
    found[0] = sketch
    solved = []
    for at in range(probes):
        value = sketch[at:at + 1, :]
        for back in range(at):
            value = value - lower[at, back] * solved[back]
        solved.append(value * inverse[at])
        found[1, at:at + 1, :] = solved[at]
    for part in range(each):
        place = pl.ds(spot_ref[1] * each + part, 1)
        sketch_ref[part:part + 1, :] = found[0, place, :]
        basis_ref[part:part + 1, :] = found[1, place, :]


def vmem():
    return pl.BlockSpec(memory_space=pltpu.VMEM)


def smem():
    return pl.BlockSpec(memory_space=pltpu.SMEM)


def params():
    return pltpu.CompilerParams(vmem_limit_bytes=56 << 20)


def filter_power(corr_lengths, height, width):
    wave_y = jnp.arange(height // 2 + 1, dtype=jnp.int32)
    wave_x = jnp.arange(width // 2 + 1, dtype=jnp.int32)
    weight_y = jnp.where((wave_y == 0) | (wave_y == height // 2), 1.0, 2.0)
    weight_x = jnp.where((wave_x == 0) | (wave_x == width // 2), 1.0, 2.0)
    down = (corr_lengths[0] * (wave_y.astype(F32) * (2.0 * math.pi / height))) ** 2
    across = (corr_lengths[1] * (wave_x.astype(F32) * (2.0 * math.pi / width))) ** 2
    root = lax.rsqrt(1.0 + down[:, None] + across[None, :])
    return jnp.sum(root * root * root * (weight_y[:, None] * weight_x[None, :]))


def send(value, axis, hop, sent):
    pairs = [(source, source ^ hop) for source in range(lax.axis_size(axis))]
    if len(sent) >= WINDOW:
        value, _ = lax.optimization_barrier((value, sent[-WINDOW]))
    return lax.ppermute(value, axis, pairs)


def exchange(blocks, sent):
    slabs = len(blocks)
    far, near = range(slabs - 1, slabs // 2 - 1, -1), range(slabs // 2 - 1, 0, -1)
    arrived = list(blocks)
    for hop in [hop for pair in zip(far, near) for hop in pair] + [far[-1]]:
        arrived[hop] = send(blocks[hop], "grid", hop, sent)
        sent.append(arrived[hop])
    return arrived


def local(probes, corr_lengths, footprints, reading_slab, reading_band, reading_tile):
    rows, each, width = probes.shape
    slabs, lanes_q = lax.axis_size("grid"), lax.axis_size("probe")
    me, lane_at = lax.axis_index("grid"), lax.axis_index("probe")
    height = rows * slabs
    short = width // RADIX
    own = width // slabs
    cut = min(LANES, own)
    chunks = own // cut
    tile = min(TILE, rows)
    halves = short // LANES
    lead, trail, back_lead, back_trail = (jnp.asarray(part) for part in dft_blocks(short))
    turn_x = jnp.asarray(twiddles(width))
    turn_y = jnp.asarray(twiddles(height).T.copy())
    me_list = jnp.stack([me, lane_at]).astype(jnp.int32)
    spot = me_list
    read_count, band_rows, tile_cols = footprints.shape
    band_count = rows // band_rows
    capacity = 2 * read_count // slabs
    share = capacity // lanes_q
    slots = slabs * capacity
    packed, place = pl.pallas_call(
        lambda *refs: pack_kernel(slabs, capacity, band_count, *refs),
        in_specs=[smem()] + [vmem()] * 4,
        out_specs=[vmem()] * 2,
        out_shape=[
            jax.ShapeDtypeStruct((slabs, share + 1, band_rows, tile_cols), BF16),
            jax.ShapeDtypeStruct((1, read_count), jnp.int32),
        ],
        scratch_shapes=[
            pltpu.VMEM((read_count * band_rows, LANES), F32),
            pltpu.VMEM((read_count, band_rows * LANES), BF16),
            pltpu.VMEM((slabs * share * band_rows, LANES), F32),
        ],
        compiler_params=params(),
        name="pack_prints",
    )(
        me_list,
        reading_slab.reshape(1, read_count),
        reading_band.reshape(1, read_count),
        reading_tile.reshape(1, read_count),
        footprints,
    )
    gathered = lax.all_to_all(packed, "grid", split_axis=0, concat_axis=0, tiled=True)
    me_list, _ = lax.optimization_barrier((me_list, packed))
    column_tiles = width // LANES
    flat = (
        probes.reshape(rows, each, column_tiles, LANES)
        .transpose(0, 2, 1, 3)
        .reshape(rows * each * column_tiles, LANES)
    )
    payload = jax.ShapeDtypeStruct((2 * rows + RADIX, cut), I16)

    def whole(shape):
        return pl.BlockSpec(shape, lambda step: (0,) * len(shape))

    sent = pl.pallas_call(
        lambda *refs: rows_kernel(slabs, chunks, *refs),
        grid=(rows // tile,),
        in_specs=[
            smem(),
            pl.BlockSpec((tile * each * column_tiles, LANES), lambda step: (step, 0)),
            whole(lead.shape),
            whole(trail.shape),
            whole(turn_x.shape),
        ],
        out_specs=[whole(payload.shape)] * (chunks * slabs),
        out_shape=[payload] * (chunks * slabs),
        scratch_shapes=[
            pltpu.VMEM((chunks, slabs, 2 * rows, cut), I16),
            pltpu.VMEM((chunks, slabs, RADIX, cut), F32),
            pltpu.VMEM((RADIX * tile, 2 * short), BF16),
            pltpu.VMEM((RADIX * tile, 2 * short), BF16),
        ],
        compiler_params=params(),
        name="rows_forward",
    )(me_list, flat, lead, trail, turn_x)

    gathered, _ = lax.optimization_barrier((gathered, sent[0]))
    gathered = lax.all_gather(gathered, "probe", axis=0, tiled=False)
    history = []
    arrived = []
    for chunk in range(chunks):
        arrived.append(exchange(sent[chunk * slabs:(chunk + 1) * slabs], history))

    halfway = []
    group = 256 // cut if cut % LANES == 0 else 1
    for chunk in range(chunks):
        results = pl.pallas_call(
            lambda *refs, chunk=chunk: columns_kernel(slabs, chunk, height, *refs),
            in_specs=[smem(), smem()]
            + [vmem()] * (slabs + 5),
            out_specs=[vmem()] * slabs,
            out_shape=[payload] * slabs,
            scratch_shapes=[
                pltpu.VMEM((slabs, 2 * rows, cut), I16),
                pltpu.VMEM((slabs, RADIX, cut), F32),
                pltpu.VMEM((2, height, cut), F32),
                pltpu.VMEM((RADIX // group, 2 * short, group * cut), BF16),
                pltpu.VMEM((RADIX // group, 2 * short, group * cut), BF16),
            ],
            compiler_params=params(),
            name="columns",
        )(
            me_list,
            corr_lengths,
            *arrived[chunk],
            lead,
            trail,
            back_lead,
            back_trail,
            turn_y,
        )
        halfway.append(list(results))

    gain = lax.rsqrt(filter_power(corr_lengths, height, width) / (height * width)) / (height * width)

    returned = []
    for results in halfway:
        returned += exchange(results, history)

    prints = gathered[:, :, :share].transpose(3, 4, 1, 0, 2).reshape(band_rows * tile_cols, slots)
    index = lax.dynamic_slice_in_dim(gathered[:, :, share, 0], me * share, share, 2)
    index = index.transpose(1, 0, 2).reshape(1, slots).astype(jnp.int32)

    group_count = slabs * lanes_q
    smoothed, values = pl.pallas_call(
        lambda *refs: finish_kernel(slabs, chunks, *refs),
        grid=(rows // tile,),
        in_specs=[smem(), smem()]
        + [whole(payload.shape)] * (chunks * slabs)
        + [
            whole(lead.shape),
            whole(trail.shape),
            whole(turn_x.shape),
            pl.BlockSpec(memory_space=pl.ANY),
            whole(index.shape),
        ],
        out_specs=[
            pl.BlockSpec((tile * each * column_tiles, LANES), lambda step: (step, 0)),
            whole((group_count, each * slots // LANES, LANES)),
        ],
        out_shape=[
            jax.ShapeDtypeStruct(flat.shape, F32),
            jax.ShapeDtypeStruct((group_count, each * slots // LANES, LANES), F32),
        ],
        scratch_shapes=[
            pltpu.VMEM((chunks, slabs, 2 * rows, cut), I16),
            pltpu.VMEM((chunks, slabs, RADIX, cut), F32),
            pltpu.VMEM((RADIX * tile, 2 * short), BF16),
            pltpu.VMEM((RADIX * tile, 2 * short), BF16),
            pltpu.VMEM((each * column_tiles, rows, LANES), F32),
            pltpu.VMEM((each * column_tiles * band_count, band_rows * tile_cols), BF16),
            pltpu.VMEM(prints.shape, BF16),
            pltpu.SemaphoreType.DMA,
        ],
        compiler_params=params(),
        name="rows_back",
    )(me_list, gain.reshape(1), *returned, back_lead, back_trail, turn_x, prints, index)
    smoothed = (
        smoothed.reshape(rows, column_tiles, each, LANES).transpose(0, 2, 1, 3).reshape(rows, each, width)
    )

    everyone = lax.all_to_all(values, ("grid", "probe"), split_axis=0, concat_axis=0, tiled=True)
    lane_of = place[0] // capacity * LANES + me * capacity % LANES + place[0] % capacity
    pick = (jnp.arange(slabs * LANES, dtype=jnp.int32)[:, None] == lane_of[None, :]).astype(BF16)
    probe_count = each * lanes_q
    sketch, factor, basis = pl.pallas_call(
        lambda *refs: small_kernel(slabs, lanes_q, each, read_count * slabs, capacity, *refs),
        in_specs=[smem(), vmem(), vmem()],
        out_specs=[vmem()] * 3,
        out_shape=[
            jax.ShapeDtypeStruct((each, read_count), F32),
            jax.ShapeDtypeStruct((probe_count, probe_count), F32),
            jax.ShapeDtypeStruct((each, read_count), F32),
        ],
        scratch_shapes=[
            pltpu.VMEM((probe_count, slabs * LANES), F32),
            pltpu.VMEM((2, probe_count, read_count), F32),
        ],
        compiler_params=params(),
        name="factor_basis",
    )(spot, everyone, pick)
    return (smoothed, sketch.T, factor, basis.T)


def solution(mesh):
    in_specs = (
        P("grid", "probe", None),
        P(),
        P("grid", None, None),
        P("grid", None),
        P("grid"),
        P("grid"),
    )
    out_specs = (P("grid", "probe", None), P("grid", "probe"), P(), P("grid", "probe"))
    return jax.shard_map(local, mesh=mesh, in_specs=in_specs, out_specs=out_specs, check_vma=False)
```

```python
import math

import jax
import jax.numpy as jnp
import ml_dtypes
import numpy as np
from jax import lax
from jax.experimental import pallas as pl
from jax.experimental.pallas import tpu as pltpu
from jax.sharding import PartitionSpec as P

RADIX = 8
STEPS = 64.0
TOP = 32700.0
TILE = 64
SUB = 16
LANES = 128
WINDOW = 5
PAD = 8
F32 = jnp.float32
BF16 = jnp.bfloat16
I16 = jnp.int16


def dft_blocks(length):
    grid = np.outer(np.arange(length), np.arange(length)) % length
    cosine, sine = np.cos(2 * np.pi * grid / length), np.sin(2 * np.pi * grid / length)
    forward = np.block([[cosine, -sine], [sine, cosine]]).astype(np.float32)
    lead = forward.astype(ml_dtypes.bfloat16)
    trail = (forward - lead.astype(np.float32)).astype(ml_dtypes.bfloat16)
    return lead, trail, lead.T.copy(), trail.T.copy()


def twiddles(length):
    short = length // RADIX
    angle = 2 * np.pi * np.outer(np.arange(RADIX), np.arange(short)) / length
    return np.concatenate([np.cos(angle), -np.sin(angle)]).astype(np.float32)


def turn(pair, sign):
    return (pair[1], -pair[0]) if sign < 0 else (-pair[1], pair[0])


def add(one, two):
    return (one[0] + two[0], one[1] + two[1])


def sub(one, two):
    return (one[0] - two[0], one[1] - two[1])


def dft8(x, sign):
    half = math.sqrt(0.5)
    a0, a1 = add(x[0], x[4]), sub(x[0], x[4])
    a2, a3 = add(x[2], x[6]), turn(sub(x[2], x[6]), sign)
    b0, b1 = add(x[1], x[5]), sub(x[1], x[5])
    b2, b3 = add(x[3], x[7]), turn(sub(x[3], x[7]), sign)
    even, odd = add(a0, a2), add(b0, b2)
    side, cross = sub(a0, a2), turn(sub(b0, b2), sign)
    c1, d1 = add(a1, a3), add(b1, b3)
    c3, d3 = sub(a1, a3), sub(b1, b3)
    t1, t3 = turn(d1, sign), turn(d3, sign)
    w1 = (half * (d1[0] + t1[0]), half * (d1[1] + t1[1]))
    w3 = (half * (t3[0] - d3[0]), half * (t3[1] - d3[1]))
    return [
        add(even, odd), add(c1, w1), add(side, cross), add(c3, w3),
        sub(even, odd), sub(c1, w1), sub(side, cross), sub(c3, w3),
    ]


def spin(pair, cosine, sine):
    return (pair[0] * cosine - pair[1] * sine, pair[0] * sine + pair[1] * cosine)


def split(value):
    lead = value.astype(BF16)
    return lead, (value - lead.astype(F32)).astype(BF16)


def dot(one, two):
    return jnp.dot(one, two, preferred_element_type=F32)


def encode(value):
    top = jnp.maximum(jnp.max(jnp.abs(value), axis=0, keepdims=True), 1e-30)
    exponent = jnp.ceil(jnp.log2(top) * STEPS)
    code = jnp.round(value * (jnp.exp2(exponent * (-1.0 / STEPS)) * TOP))
    return code.astype(jnp.int32).astype(I16), exponent


def scales(exponent):
    return jnp.exp2(exponent.astype(jnp.int32).astype(F32) * (1.0 / STEPS)) * (1.0 / TOP)


def pack_kernel(
    slabs, capacity, bands, spot_ref, target_ref, band_ref, tile_ref, prints_ref, packed, place_ref, wide, flat, thin
):
    count, band_rows, _ = prints_ref.shape
    share = packed.shape[1] - 1
    sent = slabs * share
    target = target_ref[...]
    mine = (lax.broadcasted_iota(jnp.int32, (slabs, 1), 0) == target).astype(F32)
    earlier = lax.broadcasted_iota(jnp.int32, (count, count), 0) < lax.broadcasted_iota(
        jnp.int32, (count, count), 1
    )
    before = dot(mine.astype(BF16), earlier.astype(F32).astype(BF16))
    slot = jnp.sum(before * mine, axis=0, keepdims=True).astype(jnp.int32)
    place = target * capacity + slot
    place_ref[...] = place
    order = lax.broadcasted_iota(jnp.int32, (sent, 1), 0)
    wanted = order // share * capacity + spot_ref[1] * share + order % share
    pick = (place == wanted).astype(F32).astype(BF16)
    code = (tile_ref[...] * bands + band_ref[...] + 1).astype(F32).astype(BF16)
    code = lax.dot_general(
        jnp.broadcast_to(code, (band_rows, count)), pick, (((1,), (1,)), ((), ())), preferred_element_type=F32
    )
    code = (code - 1.0).astype(BF16)
    wide[...] = prints_ref[...].astype(F32).reshape(count * band_rows, LANES)
    for row in range(band_rows):
        flat[:, row * LANES:(row + 1) * LANES] = wide[pl.ds(row, count, stride=band_rows), :].astype(BF16)
    picked = dot(pick, flat[...])
    for row in range(band_rows):
        thin[pl.ds(row, sent, stride=band_rows), :] = picked[:, row * LANES:(row + 1) * LANES]
    for slab in range(slabs):
        lines = thin[slab * share * band_rows:(slab + 1) * share * band_rows, :]
        packed[slab, :share] = lines.reshape(share, band_rows, LANES).astype(BF16)
        packed[slab, share] = code


def rows_kernel(slabs, chunks, me_ref, x_hbm, lead_ref, trail_ref, turn_ref, *rest):
    outs, (stack, marks, high, low, x_ref, arrival) = rest[: slabs * chunks], rest[slabs * chunks:]
    step, last = pl.program_id(0), pl.num_programs(0) - 1
    short = turn_ref.shape[1]
    halves, tile = short // LANES, high.shape[0] // RADIX
    rows = (outs[0].shape[0] - RADIX) // 2
    width = outs[0].shape[1]
    lines = 2 * RADIX * halves
    stride = lines + PAD

    def fetch(at):
        begin = pl.multiple_of(at * tile, SUB)
        return pltpu.make_async_copy(
            x_hbm.at[pl.ds(begin, tile)], x_ref.at[pl.ds(begin, tile), pl.ds(0, lines)], arrival.at[at]
        )

    @pl.when(step == 0)
    def _():
        for at in range(rows // tile):
            fetch(at).start()

    fetch(step).wait()
    x_flat = x_ref.reshape(rows * stride, LANES)
    for start in range(0, tile, SUB):
        for half in range(halves):
            values = []
            for n1 in range(RADIX):
                at = (step * tile + start) * stride + (n1 * halves + half) * 2
                values.append(
                    tuple(x_flat[pl.ds(at + part, SUB, stride=stride), :] for part in range(2))
                )
            mixed = dft8(values, -1)
            for k1 in range(RADIX):
                lanes = slice(half * LANES, (half + 1) * LANES)
                pair = mixed[k1]
                if k1:
                    pair = spin(
                        pair, turn_ref[k1:k1 + 1, lanes], turn_ref[RADIX + k1:RADIX + k1 + 1, lanes]
                    )
                for part in range(2):
                    at = part * short + half * LANES
                    lead, trail = split(pair[part])
                    high[k1 * tile + start:k1 * tile + start + SUB, at:at + LANES] = lead
                    low[k1 * tile + start:k1 * tile + start + SUB, at:at + LANES] = trail
    spectrum = (
        dot(high[...], lead_ref[...]) + dot(low[...], lead_ref[...]) + dot(high[...], trail_ref[...])
    )
    own = short * RADIX // slabs
    for slab in range(slabs):
        k1, base = slab * own // short, slab * own % short
        for chunk in range(chunks):
            for part in range(2):
                at = part * short + base + chunk * width
                code, exponent = encode(
                    spectrum[k1 * tile:(k1 + 1) * tile, at:at + width]
                )
                place = pl.multiple_of(part * rows + step * tile, SUB)
                stack[chunk, slab, pl.ds(place, tile), :] = code
                marks[chunk, slab, pl.ds(2 * step + part, 1), :] = exponent

    @pl.when(step == last)
    def _():
        for chunk in range(chunks):
            for hop in range(slabs):
                slab = me_ref[0] ^ hop
                out = outs[chunk * slabs + hop]
                out[:2 * rows, :] = stack[chunk, slab]
                out[2 * rows:, :] = marks[chunk, slab].astype(jnp.int32).astype(I16)


def columns_kernel(slabs, chunk, length, me_ref, corr_ref, *rest):
    me = me_ref[0]
    ins, rest = rest[:slabs], rest[slabs:]
    back_lead, back_trail, lead, trail, turn_ref = rest[:5]
    outs, (stack, scale, field, high, low) = rest[5:5 + slabs], rest[5 + slabs:]
    short = length // RADIX
    rows = stack.shape[1] // 2
    width = stack.shape[2]
    tile = min(TILE, rows)
    group = high.shape[2] // width
    for hop in range(slabs):
        stack[me ^ hop] = ins[hop][:2 * rows, :]
        scale[me ^ hop] = scales(ins[hop][2 * rows:, :])
    for start in range(0, short, SUB):
        values = []
        for n1 in range(RADIX):
            slab, row = divmod(n1 * short + start, rows)
            mark = 2 * (row // tile)
            values.append(
                tuple(
                    stack[slab, part * rows + row:part * rows + row + SUB, :].astype(jnp.int32).astype(F32)
                    * scale[slab, mark + part:mark + part + 1, :]
                    for part in range(2)
                )
            )
        mixed = dft8(values, -1)
        for k1 in range(RADIX):
            pair = mixed[k1]
            if k1:
                pair = spin(
                    pair,
                    turn_ref[start:start + SUB, k1:k1 + 1],
                    turn_ref[start:start + SUB, RADIX + k1:RADIX + k1 + 1],
                )
            at = (k1 % group) * width
            for part in range(2):
                one, two = split(pair[part])
                place = slice(part * short + start, part * short + start + SUB)
                high[k1 // group, place, at:at + width] = one
                low[k1 // group, place, at:at + width] = two
    place = me * (length // slabs) + chunk * width
    lane = place + lax.broadcasted_iota(jnp.int32, (1, width), 1)
    wave_x = (lane // short) + RADIX * (lane % short)
    wave_x = jnp.where(wave_x < length // 2, wave_x, wave_x - length).astype(F32)
    unit = 2.0 * math.pi / length
    across = (corr_ref[1] * (wave_x * unit)) ** 2 + 1.0
    count = lax.broadcasted_iota(jnp.int32, (short, 1), 0)
    for pair_at in range(RADIX // group):
        one, two = high[pair_at], low[pair_at]
        spectrum = dot(lead[...], one) + dot(lead[...], two) + dot(trail[...], one)
        for slot in range(group):
            k1 = pair_at * group + slot
            wave_y = k1 + RADIX * count
            wave_y = jnp.where(wave_y < length // 2, wave_y, wave_y - length).astype(F32)
            down = (corr_ref[0] * (wave_y * unit)) ** 2
            root = lax.rsqrt(down + across)
            shape = root * root * lax.rsqrt(root)
            lanes = slice(slot * width, (slot + 1) * width)
            for part in range(2):
                place = slice(part * short, (part + 1) * short)
                one, two = split(spectrum[place, lanes] * shape)
                high[pair_at, place, lanes] = one
                low[pair_at, place, lanes] = two
        one, two = high[pair_at], low[pair_at]
        spectrum = (
            dot(back_lead[...], one) + dot(back_lead[...], two) + dot(back_trail[...], one)
        )
        for slot in range(group):
            k1 = pair_at * group + slot
            lanes = slice(slot * width, (slot + 1) * width)
            pair = (spectrum[:short, lanes], spectrum[short:, lanes])
            if k1:
                pair = spin(
                    pair, turn_ref[:, k1:k1 + 1], -turn_ref[:, RADIX + k1:RADIX + k1 + 1]
                )
            for part in range(2):
                field[part, k1 * short:(k1 + 1) * short, :] = pair[part]
    for start in range(0, short, SUB):
        values = [
            tuple(
                field[part, k1 * short + start:k1 * short + start + SUB, :] for part in range(2)
            )
            for k1 in range(RADIX)
        ]
        mixed = dft8(values, 1)
        for n1 in range(RADIX):
            for part in range(2):
                field[part, n1 * short + start:n1 * short + start + SUB, :] = mixed[n1][part]
    for slab in range(slabs):
        for at in range(rows // tile):
            for part in range(2):
                begin = slab * rows + at * tile
                code, exponent = encode(field[part, begin:begin + tile, :])
                stack[slab, part * rows + at * tile:part * rows + (at + 1) * tile, :] = code
                scale[slab, 2 * at + part:2 * at + part + 1, :] = exponent
    for hop in range(slabs):
        outs[hop][:2 * rows, :] = stack[me ^ hop]
        outs[hop][2 * rows:, :] = scale[me ^ hop].astype(jnp.int32).astype(I16)


def finish_kernel(slabs, chunks, me_ref, gain_ref, *rest):
    ins, rest = rest[:slabs * chunks], rest[slabs * chunks:]
    lead_ref, trail_ref, turn_ref, prints_hbm, index_ref, out_hbm, value_ref = rest[:7]
    stack, scale, high, low, field, blocks, prints_ref, semaphore, out_ref, departure = rest[7:]
    step, last = pl.program_id(0), pl.num_programs(0) - 1
    short = turn_ref.shape[1]
    halves, tile = short // LANES, high.shape[0] // RADIX
    rows = stack.shape[2] // 2
    width = stack.shape[3]
    lines = 2 * RADIX * halves
    stride = lines + PAD
    out_flat = out_ref.reshape(rows * stride, LANES)
    band_rows = prints_ref.shape[0] // LANES

    @pl.when(step == 0)
    def _():
        pltpu.make_async_copy(prints_hbm, prints_ref, semaphore).start()
        for chunk in range(chunks):
            for hop in range(slabs):
                slab = me_ref[0] ^ hop
                stack[chunk, slab] = ins[chunk * slabs + hop][:2 * rows, :]
                scale[chunk, slab] = scales(ins[chunk * slabs + hop][2 * rows:, :])

    own = short * RADIX // slabs
    for slab in range(slabs):
        k1, base = slab * own // short, slab * own % short
        for chunk in range(chunks):
            for part in range(2):
                place = pl.multiple_of(part * rows + step * tile, SUB)
                value = (
                    stack[chunk, slab, pl.ds(place, tile), :].astype(jnp.int32).astype(F32)
                    * scale[chunk, slab, pl.ds(2 * step + part, 1), :]
                )
                at = part * short + base + chunk * width
                one, two = split(value)
                high[k1 * tile:(k1 + 1) * tile, at:at + width] = one
                low[k1 * tile:(k1 + 1) * tile, at:at + width] = two
    mixed = (
        dot(high[...], lead_ref[...]) + dot(low[...], lead_ref[...]) + dot(high[...], trail_ref[...])
    )
    gain = gain_ref[0]
    for start in range(0, tile, SUB):
        for half in range(halves):
            lanes = slice(half * LANES, (half + 1) * LANES)
            values = []
            for k1 in range(RADIX):
                place = slice(k1 * tile + start, k1 * tile + start + SUB)
                at = half * LANES
                pair = (mixed[place, at:at + LANES], mixed[place, short + at:short + at + LANES])
                if k1:
                    pair = spin(
                        pair, turn_ref[k1:k1 + 1, lanes], -turn_ref[RADIX + k1:RADIX + k1 + 1, lanes]
                    )
                values.append(pair)
            done = dft8(values, 1)
            for n1 in range(RADIX):
                column = n1 * halves + half
                for part in range(2):
                    value = done[n1][part] * gain
                    at = (step * tile + start) * stride + column * 2 + part
                    out_flat[pl.ds(at, SUB, stride=stride), :] = value
                    place = pl.multiple_of((step * tile + start) // band_rows * (band_rows + PAD), PAD)
                    field[part * RADIX * halves + column, pl.ds(place, SUB), :] = value

    def store(at):
        begin = pl.multiple_of(at * tile, SUB)
        return pltpu.make_async_copy(
            out_ref.at[pl.ds(begin, tile), pl.ds(0, lines)], out_hbm.at[pl.ds(begin, tile)], departure.at[at]
        )

    store(step).start()

    @pl.when(step == last)
    def _():
        bands = rows // band_rows
        count = field.shape[0]
        for column in range(count):
            for row in range(band_rows):
                piece = field[column, pl.ds(row, bands, stride=band_rows + PAD), :]
                blocks[column * bands:(column + 1) * bands, row * LANES:(row + 1) * LANES] = (
                    piece.astype(BF16)
                )
        pltpu.make_async_copy(prints_hbm, prints_ref, semaphore).wait()
        values = dot(blocks[...], prints_ref[...])
        each = count // 2 * bands
        chosen = lax.broadcasted_iota(jnp.int32, (each, 1), 0) == index_ref[...]
        tiles = index_ref.shape[1] // LANES
        for part in range(2):
            line = jnp.sum(
                jnp.where(chosen, values[part * each:(part + 1) * each, :], 0.0), axis=0, keepdims=True
            )
            for at in range(tiles):
                value_ref[0, part * tiles + at:part * tiles + at + 1, :] = (
                    line[:, at * LANES:(at + 1) * LANES]
                )
        for copy in range(1, value_ref.shape[0]):
            value_ref[copy] = value_ref[0]
        for at in range(rows // tile):
            store(at).wait()


def small_kernel(
    slabs, lanes_q, each, total, capacity, spot_ref, all_ref, pick_ref, sketch_ref, factor_ref, basis_ref,
    own, found,
):
    probes = lanes_q * each
    tiles = all_ref.shape[1] // each
    gram = {}
    for one in range(probes):
        for two in range(one + 1):
            sum_here = None
            for slab in range(slabs):
                left = all_ref[slab * lanes_q + one // each, (one % each) * tiles:(one % each + 1) * tiles, :]
                right = all_ref[slab * lanes_q + two // each, (two % each) * tiles:(two % each + 1) * tiles, :]
                term = left * right
                sum_here = term if sum_here is None else sum_here + term
            sum_here = jnp.sum(jnp.sum(sum_here, axis=0, keepdims=True), axis=1, keepdims=True)
            gram[one, two] = sum_here * (1.0 / total)
    lower, inverse = {}, {}
    for at in range(probes):
        left = gram[at, at]
        for back in range(at):
            left = left - lower[at, back] * lower[at, back]
        root = jnp.sqrt(left)
        lower[at, at] = root
        inverse[at] = 1.0 / root
        for down in range(at + 1, probes):
            value = gram[down, at]
            for back in range(at):
                value = value - lower[down, back] * lower[at, back]
            lower[down, at] = value * inverse[at]
    row = lax.broadcasted_iota(jnp.int32, (probes, probes), 0)
    column = lax.broadcasted_iota(jnp.int32, (probes, probes), 1)
    factor = jnp.zeros((probes, probes), F32)
    for one in range(probes):
        for two in range(one + 1):
            factor = jnp.where((row == two) & (column == one), lower[one, two], factor)
    factor_ref[...] = factor
    for slab in range(slabs):
        for one in range(probes):
            own[one:one + 1, slab * LANES:(slab + 1) * LANES] = all_ref[
                slab * lanes_q + one // each, pl.ds((one % each) * tiles + spot_ref[0] * capacity // LANES, 1), :
            ]
    value = own[...]
    first = value.astype(BF16)
    rest = value - first.astype(F32)
    second = rest.astype(BF16)
    third = (rest - second.astype(F32)).astype(BF16)
    sketch = dot(first, pick_ref[...]) + dot(second, pick_ref[...]) + dot(third, pick_ref[...])
    found[0] = sketch
    solved = []
    for at in range(probes):
        value = sketch[at:at + 1, :]
        for back in range(at):
            value = value - lower[at, back] * solved[back]
        solved.append(value * inverse[at])
        found[1, at:at + 1, :] = solved[at]
    for part in range(each):
        place = pl.ds(spot_ref[1] * each + part, 1)
        sketch_ref[part:part + 1, :] = found[0, place, :]
        basis_ref[part:part + 1, :] = found[1, place, :]


def vmem():
    return pl.BlockSpec(memory_space=pltpu.VMEM)


def smem():
    return pl.BlockSpec(memory_space=pltpu.SMEM)


def params():
    return pltpu.CompilerParams(vmem_limit_bytes=56 << 20)


def filter_power(corr_lengths, height, width):
    wave_y = jnp.arange(height // 2 + 1, dtype=jnp.int32)
    wave_x = jnp.arange(width // 2 + 1, dtype=jnp.int32)
    weight_y = jnp.where((wave_y == 0) | (wave_y == height // 2), 1.0, 2.0)
    weight_x = jnp.where((wave_x == 0) | (wave_x == width // 2), 1.0, 2.0)
    down = (corr_lengths[0] * (wave_y.astype(F32) * (2.0 * math.pi / height))) ** 2
    across = (corr_lengths[1] * (wave_x.astype(F32) * (2.0 * math.pi / width))) ** 2
    root = lax.rsqrt(1.0 + down[:, None] + across[None, :])
    return jnp.sum(root * root * root * (weight_y[:, None] * weight_x[None, :]))


def send(value, axis, hop, sent):
    pairs = [(source, source ^ hop) for source in range(lax.axis_size(axis))]
    if len(sent) >= WINDOW:
        value, _ = lax.optimization_barrier((value, sent[-WINDOW]))
    return lax.ppermute(value, axis, pairs)


def exchange(blocks, sent):
    slabs = len(blocks)
    far, near = range(slabs - 1, slabs // 2 - 1, -1), range(slabs // 2 - 1, 0, -1)
    arrived = list(blocks)
    for hop in [hop for pair in zip(far, near) for hop in pair] + [far[-1]]:
        arrived[hop] = send(blocks[hop], "grid", hop, sent)
        sent.append(arrived[hop])
    return arrived


def local(probes, corr_lengths, footprints, reading_slab, reading_band, reading_tile):
    rows, each, width = probes.shape
    slabs, lanes_q = lax.axis_size("grid"), lax.axis_size("probe")
    me, lane_at = lax.axis_index("grid"), lax.axis_index("probe")
    height = rows * slabs
    short = width // RADIX
    own = width // slabs
    cut = min(LANES, own)
    chunks = own // cut
    tile = min(TILE, rows)
    halves = short // LANES
    lead, trail, back_lead, back_trail = (jnp.asarray(part) for part in dft_blocks(short))
    turn_x = jnp.asarray(twiddles(width))
    turn_y = jnp.asarray(twiddles(height).T.copy())
    me_list = jnp.stack([me, lane_at]).astype(jnp.int32)
    spot = me_list
    read_count, band_rows, tile_cols = footprints.shape
    band_count = rows // band_rows
    capacity = 2 * read_count // slabs
    share = capacity // lanes_q
    slots = slabs * capacity
    packed, place = pl.pallas_call(
        lambda *refs: pack_kernel(slabs, capacity, band_count, *refs),
        in_specs=[smem()] + [vmem()] * 4,
        out_specs=[vmem()] * 2,
        out_shape=[
            jax.ShapeDtypeStruct((slabs, share + 1, band_rows, tile_cols), BF16),
            jax.ShapeDtypeStruct((1, read_count), jnp.int32),
        ],
        scratch_shapes=[
            pltpu.VMEM((read_count * band_rows, LANES), F32),
            pltpu.VMEM((read_count, band_rows * LANES), BF16),
            pltpu.VMEM((slabs * share * band_rows, LANES), F32),
        ],
        compiler_params=params(),
        name="pack_prints",
    )(
        me_list,
        reading_slab.reshape(1, read_count),
        reading_band.reshape(1, read_count),
        reading_tile.reshape(1, read_count),
        footprints,
    )
    gathered = lax.all_to_all(packed, "grid", split_axis=0, concat_axis=0, tiled=True)
    me_list, _ = lax.optimization_barrier((me_list, packed))
    column_tiles = width // LANES
    lines = each * column_tiles
    flat = (
        probes.reshape(rows, each, column_tiles, LANES).transpose(0, 2, 1, 3).reshape(rows, lines, LANES)
    )
    payload = jax.ShapeDtypeStruct((2 * rows + RADIX, cut), I16)

    def whole(shape):
        return pl.BlockSpec(shape, lambda step: (0,) * len(shape))

    sent = pl.pallas_call(
        lambda *refs: rows_kernel(slabs, chunks, *refs),
        grid=(rows // tile,),
        in_specs=[
            smem(),
            pl.BlockSpec(memory_space=pl.ANY),
            vmem(),
            vmem(),
            vmem(),
        ],
        out_specs=[vmem()] * (chunks * slabs),
        out_shape=[payload] * (chunks * slabs),
        scratch_shapes=[
            pltpu.VMEM((chunks, slabs, 2 * rows, cut), I16),
            pltpu.VMEM((chunks, slabs, RADIX, cut), F32),
            pltpu.VMEM((RADIX * tile, 2 * short), BF16),
            pltpu.VMEM((RADIX * tile, 2 * short), BF16),
            pltpu.VMEM((rows, lines + PAD, LANES), F32),
            pltpu.SemaphoreType.DMA((rows // tile,)),
        ],
        compiler_params=params(),
        name="rows_forward",
    )(me_list, flat, lead, trail, turn_x)

    history = []
    arrived = []
    for chunk in range(chunks):
        arrived.append(exchange(sent[chunk * slabs:(chunk + 1) * slabs], history))

    gathered, _ = lax.optimization_barrier((gathered, history[:3]))
    gathered = lax.all_gather(gathered, "probe", axis=0, tiled=False)
    halfway = []
    group = 256 // cut if cut % LANES == 0 else 1
    for chunk in range(chunks):
        results = pl.pallas_call(
            lambda *refs, chunk=chunk: columns_kernel(slabs, chunk, height, *refs),
            in_specs=[smem(), smem()]
            + [vmem()] * (slabs + 5),
            out_specs=[vmem()] * slabs,
            out_shape=[payload] * slabs,
            scratch_shapes=[
                pltpu.VMEM((slabs, 2 * rows, cut), I16),
                pltpu.VMEM((slabs, RADIX, cut), F32),
                pltpu.VMEM((2, height, cut), F32),
                pltpu.VMEM((RADIX // group, 2 * short, group * cut), BF16),
                pltpu.VMEM((RADIX // group, 2 * short, group * cut), BF16),
            ],
            compiler_params=params(),
            name="columns",
        )(
            me_list,
            corr_lengths,
            *arrived[chunk],
            lead,
            trail,
            back_lead,
            back_trail,
            turn_y,
        )
        halfway.append(list(results))

    gain = lax.rsqrt(filter_power(corr_lengths, height, width) / (height * width)) / (height * width)

    returned = []
    for results in halfway:
        returned += exchange(results, history)

    prints = gathered[:, :, :share].transpose(3, 4, 1, 0, 2).reshape(band_rows * tile_cols, slots)
    index = lax.dynamic_slice_in_dim(gathered[:, :, share, 0], me * share, share, 2)
    index = index.transpose(1, 0, 2).reshape(1, slots).astype(jnp.int32)

    group_count = slabs * lanes_q
    smoothed, values = pl.pallas_call(
        lambda *refs: finish_kernel(slabs, chunks, *refs),
        grid=(rows // tile,),
        in_specs=[smem(), smem()]
        + [vmem()] * (chunks * slabs)
        + [
            vmem(),
            vmem(),
            vmem(),
            pl.BlockSpec(memory_space=pl.ANY),
            vmem(),
        ],
        out_specs=[
            pl.BlockSpec(memory_space=pl.ANY),
            whole((group_count, each * slots // LANES, LANES)),
        ],
        out_shape=[
            jax.ShapeDtypeStruct(flat.shape, F32),
            jax.ShapeDtypeStruct((group_count, each * slots // LANES, LANES), F32),
        ],
        scratch_shapes=[
            pltpu.VMEM((chunks, slabs, 2 * rows, cut), I16),
            pltpu.VMEM((chunks, slabs, RADIX, cut), F32),
            pltpu.VMEM((RADIX * tile, 2 * short), BF16),
            pltpu.VMEM((RADIX * tile, 2 * short), BF16),
            pltpu.VMEM((lines, band_count * (band_rows + PAD), LANES), F32),
            pltpu.VMEM((each * column_tiles * band_count, band_rows * tile_cols), BF16),
            pltpu.VMEM(prints.shape, BF16),
            pltpu.SemaphoreType.DMA,
            pltpu.VMEM((rows, lines + PAD, LANES), F32),
            pltpu.SemaphoreType.DMA((rows // tile,)),
        ],
        compiler_params=params(),
        name="rows_back",
    )(me_list, gain.reshape(1), *returned, back_lead, back_trail, turn_x, prints, index)
    smoothed = (
        smoothed.reshape(rows, column_tiles, each, LANES).transpose(0, 2, 1, 3).reshape(rows, each, width)
    )

    everyone = lax.all_to_all(values, ("grid", "probe"), split_axis=0, concat_axis=0, tiled=True)
    lane_of = place[0] // capacity * LANES + me * capacity % LANES + place[0] % capacity
    pick = (jnp.arange(slabs * LANES, dtype=jnp.int32)[:, None] == lane_of[None, :]).astype(BF16)
    probe_count = each * lanes_q
    sketch, factor, basis = pl.pallas_call(
        lambda *refs: small_kernel(slabs, lanes_q, each, read_count * slabs, capacity, *refs),
        in_specs=[smem(), vmem(), vmem()],
        out_specs=[vmem()] * 3,
        out_shape=[
            jax.ShapeDtypeStruct((each, read_count), F32),
            jax.ShapeDtypeStruct((probe_count, probe_count), F32),
            jax.ShapeDtypeStruct((each, read_count), F32),
        ],
        scratch_shapes=[
            pltpu.VMEM((probe_count, slabs * LANES), F32),
            pltpu.VMEM((2, probe_count, read_count), F32),
        ],
        compiler_params=params(),
        name="factor_basis",
    )(spot, everyone, pick)
    return (smoothed, sketch.T, factor, basis.T)


def solution(mesh):
    in_specs = (
        P("grid", "probe", None),
        P(),
        P("grid", None, None),
        P("grid", None),
        P("grid"),
        P("grid"),
    )
    out_specs = (P("grid", "probe", None), P("grid", "probe"), P(), P("grid", "probe"))
    return jax.shard_map(local, mesh=mesh, in_specs=in_specs, out_specs=out_specs, check_vma=False)
```
